32 devices in a mesh: groups: 2 (over x), seq: 8 (over z, y), expert: 2 (over core).
Axes of the slice: x: 2, y: 2, z: 4, core: 2. Of those that a mesh axis runs over, the one named last changes fastest.
Arguments:
- queries: bfloat16 [4, 1024, 2048], P(('groups', 'expert'), 'seq'), parts along dimension 0, may hold values from -6 to 6
- key_rows: bfloat16 [4, 1024, 2048], P(('groups', 'expert'), 'seq'), parts along dimension 0, may hold values from -6 to 6
- value_rows: bfloat16 [4, 1024, 2048], P(('groups', 'expert'), 'seq'), parts along dimension 0, may hold values from -6 to 6
- head_gain: float32 [2048], replicated, may hold values from 0.25 to 1.75
- ffn_gain: float32 [2048], replicated, may hold values from 0.25 to 1.75
- expert_ids: int32 [4, 1024, 8], P(('groups', 'expert'), 'seq'), parts along dimension 0, may hold values from 0 to 15, all different within a row; in each aligned block of 128 rows (0 to 127, 128 to 255, ..., all dimensions but the last counted through in order) at most 96 rows name the same one
- router_weight: float32 [4, 1024, 8], P(('groups', 'expert'), 'seq'), parts along dimension 0, may hold values from 0.05 to 1
- w_gate: bfloat16 [16, 2048, 512], P(('seq', 'expert')), may hold values from -0.125 to 0.125
- w_up: bfloat16 [16, 2048, 512], P(('seq', 'expert')), may hold values from -0.125 to 0.125
- w_down: bfloat16 [16, 512, 2048], P(('seq', 'expert')), may hold values from -0.25 to 0.25
Outputs:
- attention: bfloat16 [4, 1024, 2048], P(('groups', 'expert'), 'seq'), parts along dimension 0
- layer_out: bfloat16 [4, 1024, 2048], P(('groups', 'expert'), 'seq'), parts along dimension 0
The draws below stay inside these ranges and needn't reach their ends.
There are 2 independent parts, one for each index of `groups`. The reference program is written for one: setup_inputs(seed, part) draws one part's arguments, and reference() takes and returns one part's arrays. A program takes and returns all parts, laid end to end along the dimension named above; an argument that names none is the same for every part. Nothing has to cross between parts.
Inputs may be any that keep to these rules, and one draw needn't show every extreme that they name: `expert_ids`: each token names 8 different experts. Among the 128 positions k * 128 to (k + 1) * 128 - 1 of one sequence no expert is named more than 96 times, and in every draw some expert is named exactly 96 times there.
All inputs are finite; a program needn't handle non-finite values.
Results may differ from the reference program's by a relative error of at most 0.0075.
Values may be sent and summed in bfloat16 or wider, within the bound.
No kernel may reach another device: no remote copies, remote signals or barrier semaphores. Data moves between devices by JAX's collectives and lax.ppermute only.
A program may use at most 128 MiB of HBM per device.

```python
import math
import jax
import jax.numpy as jnp
import numpy as np
from jax import lax

D = 2048
HEADS = 16
HEAD_DIM = 128
TOP = 8
FF = 512
TOK_DEV = 128
EXPERTS = 16
SEQS = 2
LENGTH = 1024
CAP = 96
N_SEQ = 8


def levels(key, shape, pieces, low, largest):
    def one(dim, shards_of):
        heights = jax.random.uniform(jax.random.fold_in(jax.random.fold_in(key, 6), dim), (shards_of,), jnp.float32, low / len(pieces), largest / len(pieces))
        return jnp.repeat(jnp.exp(heights), shape[dim] // shards_of).reshape((-1,) + (1,) * (len(shape) - dim - 1))

    level = one(*pieces[0])
    for cut in pieces[1:]:
        level = level * one(*cut)
    return level


def deal_out(rng, own, number, rows, count, top, bound, lean):
    order = jax.random.permutation(rng, count)
    crowded, ordinary = load_shares(count, rows * top, bound, lean, True), load_shares(count, rows * top, bound, lean, False)
    places = jnp.arange(count)

    def named(sizes, rotation):
        used = int((sizes > 0).sum())
        fixed = max(1, used // 4)
        shifted = fixed + (places - fixed + rotation * (used - fixed)) % max(1, count - fixed)
        return jnp.zeros((count,), jnp.int32).at[order[jnp.where(places < fixed, places, shifted)]].set(jnp.asarray(sizes, jnp.int32))

    sizes = jnp.where(number % 4 == 0, named(crowded, number // 4), named(ordinary, number - number // 4 - 1))
    mixed = jax.random.permutation(jax.random.fold_in(own, 3), count)
    giver, taker = mixed[0:count // 2 * 2:2], mixed[1:count // 2 * 2:2]
    margin = jnp.minimum(sizes[giver] - 1, bound - sizes[taker]) // 2
    margin = jnp.where((giver == order[0]) | (taker == order[0]) | (sizes[taker] == 0), 0, jnp.maximum(margin, 0))
    shifted = jax.random.randint(jax.random.fold_in(own, 4), (count // 2,), 0, 1 << 20) % (margin + 1)
    sizes = sizes.at[giver].add(-shifted).at[taker].add(shifted)
    members = jnp.searchsorted(jnp.cumsum(sizes), jnp.arange(rows * top), side="right").astype(jnp.int32)
    listing = members.reshape(top, rows).T
    listing = listing[jax.random.permutation(jax.random.fold_in(own, 1), rows)]
    rotation = jax.random.randint(jax.random.fold_in(own, 2), (rows, 1), 0, top)
    return jnp.take_along_axis(listing, (jnp.arange(top)[None, :] + rotation) % top, axis=1)


def load_shares(amount, total, most, skew, full):
    portions = [(1 << 20) // math.isqrt(standing ** skew) + 1 for standing in range(1, amount + 1)]
    largest = most if full else min(most, max(-(-total // amount), total * portions[0] // sum(portions)))
    least = 1 if total - largest >= amount - 1 else 0
    given, rest = [largest] + [least] * (amount - 1), total - largest - least * (amount - 1)
    while rest > 0:
        candidates = [i for i in range(1, amount) if given[i] < largest] or [i for i in range(1, amount) if given[i] < most]
        whole, remaining = sum([portions[i] for i in candidates]), rest
        for i in candidates:
            more = min(most - given[i], max(1, remaining * portions[i] // whole), rest)
            given[i] = given[i] + more
            rest = rest - more
    return np.array(given)


def scatter_about(rng, dims, spread, most, pieces=(), held_as=jnp.bfloat16):
    drawn = spread * jax.random.normal(rng, dims, jnp.float32)
    if pieces:
        drawn = drawn * levels(rng, dims, pieces, -0.22, 0.18)
    return jnp.clip(drawn, -most, most).astype(held_as)


def setup_inputs(seed: int = 0, part: int = 0) -> dict:
    splits = jax.random.split(jax.random.key(seed), 11)
    own_keys = jax.random.split(jax.random.fold_in(splits[10], part), 11)
    queries = scatter_about(own_keys[0], (SEQS, LENGTH, D), 1.0, 6.0, ((0, 2), (1, 8)))
    key_rows = scatter_about(own_keys[1], (SEQS, LENGTH, D), 1.0, 6.0, ((0, 2), (1, 8)))
    value_rows = scatter_about(own_keys[2], (SEQS, LENGTH, D), 1.0, 6.0, ((0, 2), (1, 8)))
    head_gain = jnp.clip(1.0 + 0.15 * jax.random.normal(splits[3], (D,), jnp.float32), 0.25, 1.75)
    ffn_gain = jnp.clip(1.0 + 0.15 * jax.random.normal(splits[4], (D,), jnp.float32), 0.25, 1.75)
    expert_ids_keys = jax.random.split(jax.random.fold_in(own_keys[5], 1), SEQS * LENGTH // TOK_DEV)
    expert_ids_turns = jax.random.permutation(jax.random.fold_in(own_keys[5], 3), SEQS * LENGTH // TOK_DEV)
    expert_ids = jax.vmap(lambda own, number: deal_out(jax.random.fold_in(own_keys[5], 2), own, number, TOK_DEV, EXPERTS, TOP, CAP, 2))(expert_ids_keys, expert_ids_turns).reshape((SEQS, LENGTH, TOP))
    router_weight = jnp.clip(jnp.exp(math.log(1.0) - 2.9957323 * jax.random.uniform(own_keys[6], (SEQS, LENGTH, TOP), jnp.float32) ** levels(own_keys[6], (SEQS, LENGTH, TOP), ((0, 2), (1, 8)), -0.2, 0.2)), 0.05, 1.0)
    w_gate = scatter_about(splits[7], (EXPERTS, D, FF), D ** -0.5, 0.125, ((0, 16),))
    w_up = scatter_about(splits[8], (EXPERTS, D, FF), D ** -0.5, 0.125, ((0, 16),))
    w_down = scatter_about(splits[9], (EXPERTS, FF, D), FF ** -0.5, 0.25, ((0, 16),))
    return {"queries": queries, "key_rows": key_rows, "value_rows": value_rows, "head_gain": head_gain, "ffn_gain": ffn_gain, "expert_ids": expert_ids, "router_weight": router_weight, "w_gate": w_gate, "w_up": w_up, "w_down": w_down}


highest = lax.Precision.HIGHEST
epsilon = 1e-06

def mix_heads(sequence):
    query_seq, key_seq, value_seq = sequence
    block_count = LENGTH // 64
    block_shape = (block_count, 64, HEADS, HEAD_DIM)
    query_blocks = query_seq.reshape(block_shape).astype(jnp.float32)
    key_blocks = key_seq.reshape(block_shape).astype(jnp.float32)
    value_blocks = value_seq.reshape(block_shape).astype(jnp.float32)
    causal = jnp.arange(64)[:, None] >= jnp.arange(64)[None, :]

    def advance(state, block):
        query_part, key_part, value_part = block
        scores = jnp.einsum('thd,uhd->htu', query_part, key_part, precision=highest)
        scores = jnp.where(causal, scores, 0.0)
        within = jnp.einsum('htu,uhe->the', scores, value_part, precision=highest)
        before = jnp.einsum('thd,hde->the', query_part, state, precision=highest)
        state = state + jnp.einsum('thd,the->hde', key_part, value_part, precision=highest)
        return (state, within + before)
    start_state = jnp.zeros((HEADS, HEAD_DIM, HEAD_DIM), jnp.float32)
    _, mixed = lax.scan(advance, start_state, (query_blocks, key_blocks, value_blocks))
    return mixed.reshape(LENGTH, HEADS, HEAD_DIM)

def reference(queries, key_rows, value_rows, head_gain, ffn_gain, expert_ids, router_weight, w_gate, w_up, w_down):
    heads_raw = lax.map(mix_heads, (queries, key_rows, value_rows))
    mean_square = lax.optimization_barrier(jnp.mean(heads_raw * heads_raw, axis=-1, keepdims=True))
    attention = ((heads_raw * lax.rsqrt(mean_square + epsilon)).reshape(SEQS, LENGTH, D) * head_gain).astype(jnp.bfloat16)
    attn_float = attention.astype(jnp.float32)
    feature_sq = lax.optimization_barrier(jnp.mean(attn_float * attn_float, axis=-1, keepdims=True))
    normed = (attn_float * lax.rsqrt(feature_sq + epsilon) * ffn_gain).astype(jnp.bfloat16)
    token_total = SEQS * LENGTH
    normed_flat = normed.reshape(token_total, D)
    shares = router_weight / lax.optimization_barrier(jnp.sum(router_weight, axis=-1, keepdims=True))
    share_flat = shares.reshape(token_total * TOP)
    route_flat = expert_ids.reshape(token_total * TOP)
    limit = min(token_total, SEQS * N_SEQ * CAP)

    def add_expert(mixture, packed):
        expert_index, gate_weight, up_weight, down_weight = packed
        position = jnp.nonzero(route_flat == expert_index, size=limit, fill_value=token_total * TOP)[0]
        token_index = position // TOP
        inputs = jnp.take(normed_flat, token_index, axis=0, mode='fill', fill_value=0)
        gate_part = jnp.dot(inputs, gate_weight, preferred_element_type=jnp.float32)
        up_part = jnp.dot(inputs, up_weight, preferred_element_type=jnp.float32)
        expert_hidden = (jax.nn.silu(gate_part) * up_part).astype(jnp.bfloat16)
        expert_out = jnp.dot(expert_hidden, down_weight, preferred_element_type=jnp.float32).astype(jnp.bfloat16)
        weight_rows = jnp.take(share_flat, position, mode='fill', fill_value=0.0)
        mixture = mixture.at[token_index].add(weight_rows[:, None] * expert_out.astype(jnp.float32), mode='drop')
        return (mixture, None)
    mixture_start = jnp.zeros((token_total, D), jnp.float32)
    expert_range = jnp.arange(EXPERTS, dtype=jnp.int32)
    mixture, _ = lax.scan(add_expert, mixture_start, (expert_range, w_gate, w_up, w_down))
    layer_out = (attn_float.reshape(token_total, D) + mixture).astype(jnp.bfloat16).reshape(SEQS, LENGTH, D)
    return (attention, layer_out)
```

```python
import functools

import jax
import jax.numpy as jnp
from jax import lax
from jax.experimental import pallas as pl
from jax.experimental.pallas import tpu as pltpu
from jax.sharding import PartitionSpec as P

HEAD_DIM = 128
PAD = 16

epsilon = 1e-06
f32 = jnp.float32
bf16 = jnp.bfloat16


def full(shape):
    return pl.BlockSpec(shape, lambda *_: (0,) * len(shape))


def dot(a, b, dims=((1,), (0,))):
    return lax.dot_general(a, b, (dims, ((), ())), preferred_element_type=f32)


def state_kernel(core_ref, ids_ref, rw_ref, k_ref, v_ref, send_ref):
    n_seq, block, _ = send_ref.shape
    part = block - PAD
    step = min(part, HEAD_DIM)
    for h in range(k_ref.shape[1] // HEAD_DIM):
        cols = slice(h * HEAD_DIM, (h + 1) * HEAD_DIM)
        state = dot(k_ref[:, cols], v_ref[:, cols], ((0,), (0,))).astype(bf16)
        for r in range(0, HEAD_DIM, step):
            row = h * HEAD_DIM + r
            send_ref[row // part, row % part : row % part + step, :] = state[r : r + step]
    core = core_ref[0]
    ids = ids_ref[...]
    shares = rw_ref[...] / jnp.sum(rw_ref[...], axis=0, keepdims=True)
    zero = jnp.zeros((PAD - 4, ids.shape[1]), f32)
    for s in range(n_seq):
        own = jnp.sum(jnp.where(ids == 2 * s + core, shares, 0.0), axis=0, keepdims=True)
        other = jnp.sum(jnp.where(ids == 2 * s + 1 - core, shares, 0.0), axis=0, keepdims=True)
        both = jnp.concatenate([own, other], axis=0)
        high = both.astype(bf16).astype(f32)
        rows = jnp.concatenate([high, both - high, zero], axis=0)
        send_ref[s, part:, :] = rows.astype(bf16)


def prefix_kernel(got_ref, back_ref):
    n_seq, part, width = back_ref.shape
    total = jnp.zeros((part, width), f32)
    for s in range(n_seq):
        back_ref[s] = total.astype(bf16)
        if s < n_seq - 1:
            total = total + got_ref[s, :part, :].astype(f32)


def attention_kernel(q_ref, k_ref, v_ref, p_ref, hg_ref, fg_ref, att_ref, normed_ref):
    rows, width = q_ref.shape
    causal = lax.broadcasted_iota(jnp.int32, (rows, rows), 0) >= lax.broadcasted_iota(
        jnp.int32, (rows, rows), 1
    )
    feature_sq = jnp.zeros((rows, HEAD_DIM), f32)
    for h in range(width // HEAD_DIM):
        cols = slice(h * HEAD_DIM, (h + 1) * HEAD_DIM)
        q, v = q_ref[:, cols], v_ref[:, cols]
        scores = jnp.where(causal, dot(q, k_ref[:, cols], ((1,), (1,))), 0.0)
        high = scores.astype(bf16)
        low = (scores - high.astype(f32)).astype(bf16)
        raw = dot(high, v) + dot(low, v) + dot(q, p_ref[cols, :])
        mean_square = jnp.mean(raw * raw, axis=-1, keepdims=True)
        att = (raw * lax.rsqrt(mean_square + epsilon) * hg_ref[:, cols]).astype(bf16)
        att_ref[:, cols] = att
        att = att.astype(f32)
        feature_sq = feature_sq + att * att
    scale = lax.rsqrt(jnp.sum(feature_sq, axis=-1, keepdims=True) / width + epsilon)
    for h in range(width // HEAD_DIM):
        cols = slice(h * HEAD_DIM, (h + 1) * HEAD_DIM)
        normed_ref[:, cols] = (att_ref[:, cols].astype(f32) * scale * fg_ref[:, cols]).astype(bf16)


def expert_kernel(src_ref, x_ref, w_ref, g0, u0, d0, g1, u1, d1, out_ref, acc_ref):
    del src_ref
    step = pl.program_id(0)
    shares = w_ref[0].astype(f32)
    shares = jnp.transpose(shares[0:8, :])
    x = x_ref[...]
    total = None
    for e, (g, u, d) in enumerate(((g0, u0, d0), (g1, u1, d1))):
        gate = dot(x, g[...])
        up = dot(x, u[...])
        share = shares[:, e : e + 1] + shares[:, e + 2 : e + 3]
        hidden = (gate / (1.0 + jnp.exp(-gate)) * up * share).astype(bf16)
        part = dot(hidden, d[...])
        total = part if total is None else total + part

    @pl.when(step == 0)
    def _():
        acc_ref[...] = total

    @pl.when(step > 0)
    def _():
        acc_ref[...] += total

    @pl.when(step == pl.num_programs(0) - 1)
    def _():
        out_ref[...] = acc_ref[...].astype(bf16)


def run_experts(src, x, shares, own, other):
    rows, width = x.shape
    hidden = own[0].shape[1]
    chunk = min(hidden, 256)
    weight_specs = [
        pl.BlockSpec((width, chunk), lambda j, s: (0, j)),
        pl.BlockSpec((width, chunk), lambda j, s: (0, j)),
        pl.BlockSpec((chunk, width), lambda j, s: (j, 0)),
    ]
    return pl.pallas_call(
        expert_kernel,
        grid_spec=pltpu.PrefetchScalarGridSpec(
            num_scalar_prefetch=1,
            grid=(hidden // chunk,),
            in_specs=[
                pl.BlockSpec((rows, width), lambda j, s: (0, 0)),
                pl.BlockSpec((1,) + shares.shape[1:], lambda j, s: (s[0], 0, 0)),
            ]
            + weight_specs * 2,
            out_specs=pl.BlockSpec((rows, width), lambda j, s: (0, 0)),
            scratch_shapes=[pltpu.VMEM((rows, width), f32)],
        ),
        out_shape=jax.ShapeDtypeStruct((rows, width), bf16),
        cost_estimate=pl.CostEstimate(
            flops=12 * rows * width * hidden,
            bytes_accessed=12 * width * hidden + 4 * rows * width,
            transcendentals=2 * rows * hidden,
        ),
        name="experts",
    )(src, x, shares, *own, *other)


def ring_of(n_seq):
    return list(range(0, n_seq, 2)) + list(range(n_seq - 1, 0, -2)) if n_seq > 1 else [0]


def per_device(
    n_seq,
    queries,
    key_rows,
    value_rows,
    head_gain,
    ffn_gain,
    expert_ids,
    router_weight,
    w_gate,
    w_up,
    w_down,
):
    _, rows, width = queries.shape
    q, k, v = queries[0], key_rows[0], value_rows[0]
    own = (w_gate[0], w_up[0], w_down[0])
    other = tuple(lax.ppermute(w, "expert", [(0, 1), (1, 0)]) for w in own)
    seq, core = lax.axis_index("seq"), lax.axis_index("expert")

    ring = ring_of(n_seq)
    hops = []
    for i, s in enumerate(ring):
        hops.append((2 * s, 2 * ring[(i + 1) % n_seq]))
        hops.append((2 * s + 1, 2 * ring[i - 1] + 1))
    place = [0] * n_seq
    for i, s in enumerate(ring):
        place[s] = i
    mine = jnp.asarray(place, jnp.int32)[seq]
    behind = jnp.where(core == 0, -1, 1) * jnp.arange(n_seq, dtype=jnp.int32)
    sources = jnp.asarray(ring, jnp.int32)[(mine + behind) % n_seq]

    def hop(value):
        return lax.ppermute(value, ("seq", "expert"), hops)

    part = width // n_seq
    send = pl.pallas_call(
        state_kernel,
        in_specs=[pl.BlockSpec(memory_space=pltpu.SMEM)] + [pl.BlockSpec(memory_space=pltpu.VMEM)] * 4,
        out_shape=jax.ShapeDtypeStruct((n_seq, part + PAD, HEAD_DIM), bf16),
        name="states",
    )(core.reshape(1), expert_ids[0].T, router_weight[0].T, k, v)
    got = lax.all_to_all(send, "seq", split_axis=0, concat_axis=0, tiled=True)
    back = pl.pallas_call(
        prefix_kernel,
        out_shape=jax.ShapeDtypeStruct((n_seq, part, HEAD_DIM), bf16),
        name="prefix",
    )(got)
    carried = lax.all_to_all(back, "seq", split_axis=0, concat_axis=0, tiled=True)
    attention, normed = pl.pallas_call(
        attention_kernel,
        out_shape=[jax.ShapeDtypeStruct((rows, width), bf16)] * 2,
        name="attend",
    )(
        q,
        k,
        v,
        carried.reshape(width, HEAD_DIM),
        head_gain.reshape(1, width),
        ffn_gain.reshape(1, width),
    )
    shares = got[:, part:, :]

    held, partial, first = normed, None, None
    for step in range(n_seq):
        following = hop(held) if step < n_seq - 1 else None
        result = run_experts(sources[step : step + 1], held, shares, own, other)
        if step == 0:
            first = result
        elif step == 1:
            partial = result
        else:
            partial = (hop(partial).astype(f32) + result.astype(f32)).astype(bf16)
        held = following
    if n_seq > 1:
        mixture = hop(partial).astype(f32) + first.astype(f32)
    else:
        mixture = first.astype(f32)
    layer_out = (attention.astype(f32) + mixture).astype(bf16)
    return attention[None], layer_out[None]


def solution(mesh):
    tokens = P(("groups", "expert"), "seq", None)
    experts = P(("seq", "expert"), None, None)
    return jax.shard_map(
        functools.partial(per_device, mesh.shape["seq"]),
        mesh=mesh,
        in_specs=(tokens, tokens, tokens, P(), P(), tokens, tokens, experts, experts, experts),
        out_specs=(tokens, tokens),
        check_vma=False,
    )
```

```python
import functools

import jax
import jax.numpy as jnp
from jax import lax
from jax.experimental import pallas as pl
from jax.experimental.pallas import tpu as pltpu
from jax.sharding import PartitionSpec as P

HEAD_DIM = 128
PAD = 16

epsilon = 1e-06
f32 = jnp.float32
bf16 = jnp.bfloat16


VMEM = pl.BlockSpec(memory_space=pltpu.VMEM)
SMEM = pl.BlockSpec(memory_space=pltpu.SMEM)
SMALL = pltpu.CompilerParams(vmem_limit_bytes=16 << 20)


def dot(a, b, dims=((1,), (0,))):
    return lax.dot_general(a, b, (dims, ((), ())), preferred_element_type=f32)


def state_kernel(core_ref, ids_ref, rw_ref, k_ref, v_ref, send_ref):
    n_seq, block, _ = send_ref.shape
    part = block - PAD
    step = min(part, HEAD_DIM)
    for h in range(k_ref.shape[1] // HEAD_DIM):
        cols = slice(h * HEAD_DIM, (h + 1) * HEAD_DIM)
        state = dot(k_ref[:, cols], v_ref[:, cols], ((0,), (0,))).astype(bf16)
        for r in range(0, HEAD_DIM, step):
            row = h * HEAD_DIM + r
            send_ref[row // part, row % part : row % part + step, :] = state[r : r + step]
    core = core_ref[0]
    ids = ids_ref[...]
    shares = rw_ref[...] / jnp.sum(rw_ref[...], axis=0, keepdims=True)
    zero = jnp.zeros((PAD - 4, ids.shape[1]), f32)
    for s in range(n_seq):
        own = jnp.sum(jnp.where(ids == 2 * s + core, shares, 0.0), axis=0, keepdims=True)
        other = jnp.sum(jnp.where(ids == 2 * s + 1 - core, shares, 0.0), axis=0, keepdims=True)
        both = jnp.concatenate([own, other], axis=0)
        high = both.astype(bf16).astype(f32)
        rows = jnp.concatenate([high, both - high, zero], axis=0)
        send_ref[s, part:, :] = rows.astype(bf16)


def prefix_kernel(got_ref, back_ref):
    n_seq, part, width = back_ref.shape
    total = jnp.zeros((part, width), f32)
    for s in range(n_seq):
        back_ref[s] = total.astype(bf16)
        if s < n_seq - 1:
            total = total + got_ref[s, :part, :].astype(f32)


def attention_kernel(q_ref, k_ref, v_ref, p_ref, hg_ref, fg_ref, att_ref, normed_ref):
    rows, width = q_ref.shape
    causal = lax.broadcasted_iota(jnp.int32, (rows, rows), 0) >= lax.broadcasted_iota(
        jnp.int32, (rows, rows), 1
    )
    feature_sq = jnp.zeros((rows, HEAD_DIM), f32)
    for h in range(width // HEAD_DIM):
        cols = slice(h * HEAD_DIM, (h + 1) * HEAD_DIM)
        q, v = q_ref[:, cols], v_ref[:, cols]
        scores = jnp.where(causal, dot(q, k_ref[:, cols], ((1,), (1,))), 0.0)
        high = scores.astype(bf16)
        low = (scores - high.astype(f32)).astype(bf16)
        raw = dot(high, v) + dot(low, v) + dot(q, p_ref[cols, :])
        mean_square = jnp.mean(raw * raw, axis=-1, keepdims=True)
        att = (raw * lax.rsqrt(mean_square + epsilon) * hg_ref[:, cols]).astype(bf16)
        att_ref[:, cols] = att
        att = att.astype(f32)
        feature_sq = feature_sq + att * att
    scale = lax.rsqrt(jnp.sum(feature_sq, axis=-1, keepdims=True) / width + epsilon)
    for h in range(width // HEAD_DIM):
        cols = slice(h * HEAD_DIM, (h + 1) * HEAD_DIM)
        normed_ref[:, cols] = (att_ref[:, cols].astype(f32) * scale * fg_ref[:, cols]).astype(bf16)


def expert_kernel(src_ref, x_ref, w_ref, g0, u0, d0, g1, u1, d1, out_ref):
    shares = jnp.transpose(w_ref[src_ref[0]][0:8, :].astype(f32))
    x = x_ref[...]
    total = None
    for e, (g, u, d) in enumerate(((g0, u0, d0), (g1, u1, d1))):
        gate = dot(x, g[...])
        up = dot(x, u[...])
        share = shares[:, e : e + 1] + shares[:, e + 2 : e + 3]
        hidden = (gate / (1.0 + jnp.exp(-gate)) * up * share).astype(bf16)
        part = dot(hidden, d[...])
        total = part if total is None else total + part
    out_ref[...] = total.astype(bf16)


def run_experts(src, x, shares, own, other):
    rows, width = x.shape
    hidden = own[0].shape[1]
    return pl.pallas_call(
        expert_kernel,
        in_specs=[SMEM] + [VMEM] * 8,
        out_specs=VMEM,
        out_shape=jax.ShapeDtypeStruct((rows, width), bf16),
        compiler_params=pltpu.CompilerParams(vmem_limit_bytes=24 << 20),
        cost_estimate=pl.CostEstimate(
            flops=12 * rows * width * hidden,
            bytes_accessed=4 * rows * width,
            transcendentals=2 * rows * hidden,
        ),
        name="experts",
    )(src, x, shares, *own, *other)


def ring_of(n_seq):
    return list(range(0, n_seq, 2)) + list(range(n_seq - 1, 0, -2)) if n_seq > 1 else [0]


def per_device(
    n_seq,
    queries,
    key_rows,
    value_rows,
    head_gain,
    ffn_gain,
    expert_ids,
    router_weight,
    w_gate,
    w_up,
    w_down,
):
    _, rows, width = queries.shape
    q, k, v = queries[0], key_rows[0], value_rows[0]
    own = (w_gate[0], w_up[0], w_down[0])
    other = tuple(lax.ppermute(w, "expert", [(0, 1), (1, 0)]) for w in own)
    seq, core = lax.axis_index("seq"), lax.axis_index("expert")

    ring = ring_of(n_seq)
    hops = []
    for i, s in enumerate(ring):
        hops.append((2 * s, 2 * ring[(i + 1) % n_seq]))
        hops.append((2 * s + 1, 2 * ring[i - 1] + 1))
    place = [0] * n_seq
    for i, s in enumerate(ring):
        place[s] = i
    mine = jnp.asarray(place, jnp.int32)[seq]
    behind = jnp.where(core == 0, -1, 1) * jnp.arange(n_seq, dtype=jnp.int32)
    sources = jnp.asarray(ring, jnp.int32)[(mine + behind) % n_seq]

    def hop(value):
        return lax.ppermute(value, ("seq", "expert"), hops)

    part = width // n_seq
    send = pl.pallas_call(
        state_kernel,
        in_specs=[SMEM] + [VMEM] * 4,
        out_specs=VMEM,
        compiler_params=SMALL,
        out_shape=jax.ShapeDtypeStruct((n_seq, part + PAD, HEAD_DIM), bf16),
        name="states",
    )(core.reshape(1), expert_ids[0].T, router_weight[0].T, k, v)
    got = lax.all_to_all(send, "seq", split_axis=0, concat_axis=0, tiled=True)
    back = pl.pallas_call(
        prefix_kernel,
        in_specs=[VMEM],
        out_specs=VMEM,
        compiler_params=SMALL,
        out_shape=jax.ShapeDtypeStruct((n_seq, part, HEAD_DIM), bf16),
        name="prefix",
    )(got)
    carried = lax.all_to_all(back, "seq", split_axis=0, concat_axis=0, tiled=True)
    attention, normed = pl.pallas_call(
        attention_kernel,
        in_specs=[VMEM] * 6,
        out_specs=[VMEM] * 2,
        compiler_params=SMALL,
        out_shape=[jax.ShapeDtypeStruct((rows, width), bf16)] * 2,
        name="attend",
    )(
        q,
        k,
        v,
        carried.reshape(width, HEAD_DIM),
        head_gain.reshape(1, width),
        ffn_gain.reshape(1, width),
    )
    shares = got[:, part:, :]

    held, partial, first = normed, None, None
    for step in range(n_seq):
        following = hop(held) if step < n_seq - 1 else None
        result = run_experts(sources[step : step + 1], held, shares, own, other)
        if step == 0:
            first = result
        elif step == 1:
            partial = result
        else:
            partial = (hop(partial).astype(f32) + result.astype(f32)).astype(bf16)
        held = following
    if n_seq > 1:
        mixture = hop(partial).astype(f32) + first.astype(f32)
    else:
        mixture = first.astype(f32)
    layer_out = (attention.astype(f32) + mixture).astype(bf16)
    return attention[None], layer_out[None]


def solution(mesh):
    tokens = P(("groups", "expert"), "seq", None)
    experts = P(("seq", "expert"), None, None)
    return jax.shard_map(
        functools.partial(per_device, mesh.shape["seq"]),
        mesh=mesh,
        in_specs=(tokens, tokens, tokens, P(), P(), tokens, tokens, experts, experts, experts),
        out_specs=(tokens, tokens),
        check_vma=False,
    )
```

```python
import functools

import jax
import jax.numpy as jnp
from jax import lax
from jax.experimental import pallas as pl
from jax.experimental.pallas import tpu as pltpu
from jax.sharding import PartitionSpec as P

HEAD_DIM = 128
PAD = 16
CHUNKS = 4

epsilon = 1e-06
f32 = jnp.float32
bf16 = jnp.bfloat16


VMEM = pl.BlockSpec(memory_space=pltpu.VMEM)
HBM = pl.BlockSpec(memory_space=pltpu.HBM)
SMEM = pl.BlockSpec(memory_space=pltpu.SMEM)
SMALL = pltpu.CompilerParams(vmem_limit_bytes=16 << 20)


def dot(a, b, dims=((1,), (0,))):
    return lax.dot_general(a, b, (dims, ((), ())), preferred_element_type=f32)


def state_kernel(n_seq, at_ref, ids_hbm, rw_hbm, k_hbm, v_hbm, *refs):
    sends, (state_ref, ids_ref, rw_ref, k_ref, v_ref, sems) = refs[:n_seq], refs[n_seq:]
    width = k_ref.shape[1]
    part = width // n_seq
    chunk = width // CHUNKS
    copies = []
    for c in range(CHUNKS):
        cols = slice(c * chunk, (c + 1) * chunk)
        for i, (src, dst) in enumerate(((k_hbm, k_ref), (v_hbm, v_ref))):
            copies.append(pltpu.make_async_copy(src.at[:, cols], dst.at[:, cols], sems.at[2 * c + i]))
    copies.append(pltpu.make_async_copy(ids_hbm, ids_ref, sems.at[2 * CHUNKS]))
    copies.append(pltpu.make_async_copy(rw_hbm, rw_ref, sems.at[2 * CHUNKS + 1]))
    for copy in copies:
        copy.start()
    for c in range(CHUNKS):
        copies[2 * c].wait()
        copies[2 * c + 1].wait()
        for h in range(c * chunk // HEAD_DIM, (c + 1) * chunk // HEAD_DIM):
            cols = slice(h * HEAD_DIM, (h + 1) * HEAD_DIM)
            state_ref[cols, :] = dot(k_ref[:, cols], v_ref[:, cols], ((0,), (0,))).astype(bf16)
    copies[-2].wait()
    copies[-1].wait()
    seq, core = at_ref[0], at_ref[1]
    ids = ids_ref[...]
    shares = rw_ref[...] / jnp.sum(rw_ref[...], axis=0, keepdims=True)
    zero = jnp.zeros((PAD - 4, ids.shape[1]), f32)
    for r, send_ref in enumerate(sends):
        s = lax.rem(seq + r, n_seq)
        send_ref[:part, :] = state_ref[pl.ds(pl.multiple_of(s * part, part), part), :]
        own = jnp.sum(jnp.where(ids == 2 * s + core, shares, 0.0), axis=0, keepdims=True)
        other = jnp.sum(jnp.where(ids == 2 * s + 1 - core, shares, 0.0), axis=0, keepdims=True)
        both = jnp.concatenate([own, other], axis=0)
        high = both.astype(bf16).astype(f32)
        rows = jnp.concatenate([high, both - high, zero], axis=0)
        send_ref[part:, :] = rows.astype(bf16)


def prefix_kernel(n_seq, at_ref, *refs):
    gots, backs, shares_ref = refs[:n_seq], refs[n_seq:-1], refs[-1]
    part = backs[0].shape[0]
    seq = at_ref[0]
    total = jnp.zeros(backs[0].shape, f32)
    for r in range(n_seq):
        total = total + jnp.where(r <= seq, gots[r][:part, :].astype(f32), 0.0)
    for r in reversed(range(n_seq)):
        total = jnp.where(r == seq, 0.0, total)
        backs[r][...] = total.astype(bf16)
        total = total + gots[r][:part, :].astype(f32)
        terms = gots[r][part:, :].astype(f32)
        shares_ref[lax.rem(seq + n_seq - r, n_seq)] = terms[0:8] + terms[2:10]


def attention_kernel(n_seq, at_ref, q_ref, k_ref, v_ref, hg_ref, fg_ref, *refs):
    carried, (att_ref, normed_ref, p_ref) = refs[:n_seq], refs[n_seq:]
    rows, width = q_ref.shape
    part = width // n_seq
    for r in range(n_seq):
        s = lax.rem(at_ref[0] + r, n_seq)
        p_ref[pl.ds(pl.multiple_of(s * part, part), part), :] = carried[r][...]
    causal = lax.broadcasted_iota(jnp.int32, (rows, rows), 0) >= lax.broadcasted_iota(
        jnp.int32, (rows, rows), 1
    )
    feature_sq = jnp.zeros((rows, HEAD_DIM), f32)
    for h in range(width // HEAD_DIM):
        cols = slice(h * HEAD_DIM, (h + 1) * HEAD_DIM)
        q, v = q_ref[:, cols], v_ref[:, cols]
        scores = jnp.where(causal, dot(q, k_ref[:, cols], ((1,), (1,))), 0.0)
        high = scores.astype(bf16)
        low = (scores - high.astype(f32)).astype(bf16)
        raw = dot(high, v) + dot(low, v) + dot(q, p_ref[cols, :])
        mean_square = jnp.mean(raw * raw, axis=-1, keepdims=True)
        att = (raw * lax.rsqrt(mean_square + epsilon) * hg_ref[:, cols]).astype(bf16)
        att_ref[:, cols] = att
        att = att.astype(f32)
        feature_sq = feature_sq + att * att
    scale = lax.rsqrt(jnp.sum(feature_sq, axis=-1, keepdims=True) / width + epsilon)
    for h in range(width // HEAD_DIM):
        cols = slice(h * HEAD_DIM, (h + 1) * HEAD_DIM)
        normed_ref[:, cols] = (att_ref[:, cols].astype(f32) * scale * fg_ref[:, cols]).astype(bf16)


def expert_kernel(hop, at_ref, x_ref, w_ref, g0, u0, d0, g1, u1, d1, out_ref):
    n_seq = w_ref.shape[0]
    seq, core = at_ref[0], at_ref[1]
    last = n_seq - 1
    place = jnp.where(seq % 2 == 0, seq // 2, last - seq // 2)
    place = lax.rem(place + jnp.where(core == 0, n_seq - hop, hop), n_seq)
    source = jnp.where(2 * place < n_seq, 2 * place, 2 * (last - place) + 1)
    shares = jnp.transpose(w_ref[source])
    x = x_ref[...]
    total = None
    for e, (g, u, d) in enumerate(((g0, u0, d0), (g1, u1, d1))):
        gate = dot(x, g[...])
        up = dot(x, u[...])
        hidden = (gate / (1.0 + jnp.exp(-gate)) * up * shares[:, e : e + 1]).astype(bf16)
        part = dot(hidden, d[...])
        total = part if total is None else total + part
    out_ref[...] = total.astype(bf16)


def run_experts(hop, at, x, shares, weights):
    rows, width = x.shape
    hidden = weights[0].shape[1]
    return pl.pallas_call(
        functools.partial(expert_kernel, hop),
        in_specs=[SMEM] + [VMEM] * 8,
        out_specs=VMEM,
        out_shape=jax.ShapeDtypeStruct((rows, width), bf16),
        compiler_params=pltpu.CompilerParams(vmem_limit_bytes=24 << 20),
        cost_estimate=pl.CostEstimate(
            flops=12 * rows * width * hidden,
            bytes_accessed=4 * rows * width,
            transcendentals=2 * rows * hidden,
        ),
        name="experts",
    )(at, x, shares, *weights)


def in_hbm(*arrays):
    return [pltpu.with_memory_space_constraint(a, pltpu.HBM) for a in arrays]


def load_kernel(count, after_ref, *refs):
    del after_ref
    sems = refs[-1]
    copies = [pltpu.make_async_copy(refs[i], refs[count + i], sems.at[i]) for i in range(count)]
    for copy in copies:
        copy.start()
    for copy in copies:
        copy.wait()


def load(after, *arrays):
    arrays = in_hbm(*arrays)
    count = len(arrays)
    size = sum(a.size * a.dtype.itemsize for a in arrays)
    return pl.pallas_call(
        functools.partial(load_kernel, count),
        in_specs=[HBM] * (count + 1),
        out_specs=[VMEM] * count,
        out_shape=[jax.ShapeDtypeStruct(a.shape, a.dtype) for a in arrays],
        scratch_shapes=[pltpu.SemaphoreType.DMA((count,))],
        compiler_params=pltpu.CompilerParams(vmem_limit_bytes=1 << 20),
        cost_estimate=pl.CostEstimate(flops=0, bytes_accessed=size, transcendentals=0),
        name="load",
    )(after, *arrays)


def ring_of(n_seq):
    return list(range(0, n_seq, 2)) + list(range(n_seq - 1, 0, -2)) if n_seq > 1 else [0]


def per_device(
    n_seq,
    queries,
    key_rows,
    value_rows,
    head_gain,
    ffn_gain,
    expert_ids,
    router_weight,
    w_gate,
    w_up,
    w_down,
):
    _, rows, width = queries.shape
    q, k, v = queries[0], key_rows[0], value_rows[0]
    own = (w_gate[0], w_up[0], w_down[0])
    other = tuple(lax.ppermute(w, "expert", [(0, 1), (1, 0)]) for w in own)
    at = jnp.stack([lax.axis_index("seq"), lax.axis_index("expert")])

    ring = ring_of(n_seq)
    hops = []
    for i, s in enumerate(ring):
        hops.append((2 * s, 2 * ring[(i + 1) % n_seq]))
        hops.append((2 * s + 1, 2 * ring[i - 1] + 1))

    def hop(value):
        return lax.ppermute(value, ("seq", "expert"), hops)

    def along(blocks, sign):
        return [blocks[0]] + [
            lax.ppermute(blocks[r], "seq", [(s, (s + sign * r) % n_seq) for s in range(n_seq)])
            for r in range(1, n_seq)
        ]

    part = width // n_seq
    sends = pl.pallas_call(
        functools.partial(state_kernel, n_seq),
        in_specs=[SMEM] + [HBM] * 4,
        out_specs=[VMEM] * n_seq,
        scratch_shapes=[
            pltpu.VMEM((width, HEAD_DIM), bf16),
            pltpu.VMEM(expert_ids.shape[:0:-1], jnp.int32),
            pltpu.VMEM(expert_ids.shape[:0:-1], f32),
            pltpu.VMEM((rows, width), bf16),
            pltpu.VMEM((rows, width), bf16),
            pltpu.SemaphoreType.DMA((2 * CHUNKS + 2,)),
        ],
        compiler_params=SMALL,
        out_shape=[jax.ShapeDtypeStruct((part + PAD, HEAD_DIM), bf16)] * n_seq,
        name="states",
    )(at, *in_hbm(expert_ids[0].T, router_weight[0].T, k, v))
    *backs, shares = pl.pallas_call(
        functools.partial(prefix_kernel, n_seq),
        in_specs=[SMEM] + [VMEM] * n_seq,
        out_specs=[VMEM] * (n_seq + 1),
        compiler_params=SMALL,
        out_shape=[jax.ShapeDtypeStruct((part, HEAD_DIM), bf16)] * n_seq
        + [jax.ShapeDtypeStruct((n_seq, 8, rows), f32)],
        name="prefix",
    )(at, *along(sends, 1))
    arrays = (q, k, v, head_gain.reshape(1, width), ffn_gain.reshape(1, width))
    *arrays, g0, u0, d0, g1, u1, d1 = load(backs[0], *arrays, *own, *other)
    weights = (g0, u0, d0, g1, u1, d1)
    attention, normed = pl.pallas_call(
        functools.partial(attention_kernel, n_seq),
        in_specs=[SMEM] + [VMEM] * (n_seq + 5),
        out_specs=[VMEM] * 2,
        scratch_shapes=[pltpu.VMEM((width, HEAD_DIM), bf16)],
        compiler_params=SMALL,
        out_shape=[jax.ShapeDtypeStruct((rows, width), bf16)] * 2,
        name="attend",
    )(at, *arrays, *along(backs, -1))
    held, partial, first = normed, None, None
    for step in range(n_seq):
        following = hop(held) if step < n_seq - 1 else None
        result = run_experts(step, at, held, shares, weights)
        if step == 0:
            first = result
        elif step == 1:
            partial = result
        else:
            partial = (hop(partial).astype(f32) + result.astype(f32)).astype(bf16)
        held = following
    if n_seq > 1:
        mixture = hop(partial).astype(f32) + first.astype(f32)
    else:
        mixture = first.astype(f32)
    layer_out = (attention.astype(f32) + mixture).astype(bf16)
    return attention[None], layer_out[None]


def solution(mesh):
    tokens = P(("groups", "expert"), "seq", None)
    experts = P(("seq", "expert"), None, None)
    return jax.shard_map(
        functools.partial(per_device, mesh.shape["seq"]),
        mesh=mesh,
        in_specs=(tokens, tokens, tokens, P(), P(), tokens, tokens, experts, experts, experts),
        out_specs=(tokens, tokens),
        check_vma=False,
    )
```

```python
import functools

import jax
import jax.numpy as jnp
from jax import lax
from jax.experimental import pallas as pl
from jax.experimental.pallas import tpu as pltpu
from jax.sharding import PartitionSpec as P

HEAD_DIM = 128
PAD = 16
CHUNKS = 4

epsilon = 1e-06
f32 = jnp.float32
bf16 = jnp.bfloat16


VMEM = pl.BlockSpec(memory_space=pltpu.VMEM)
HBM = pl.BlockSpec(memory_space=pltpu.HBM)
SMEM = pl.BlockSpec(memory_space=pltpu.SMEM)
SMALL = pltpu.CompilerParams(vmem_limit_bytes=16 << 20)


def dot(a, b, dims=((1,), (0,))):
    return lax.dot_general(a, b, (dims, ((), ())), preferred_element_type=f32)


def state_kernel(half, at_ref, ids_hbm, rw_hbm, k_hbm, v_hbm, *refs):
    sends, (state_ref, ids_ref, rw_ref, k_ref, v_ref, sems) = refs[:half], refs[half:]
    width = k_ref.shape[1]
    part = width // half
    chunk = width // CHUNKS
    copies = []
    for c in range(CHUNKS):
        cols = slice(c * chunk, (c + 1) * chunk)
        for i, (src, dst) in enumerate(((k_hbm, k_ref), (v_hbm, v_ref))):
            copies.append(pltpu.make_async_copy(src.at[:, cols], dst.at[:, cols], sems.at[2 * c + i]))
    copies.append(pltpu.make_async_copy(ids_hbm, ids_ref, sems.at[2 * CHUNKS]))
    copies.append(pltpu.make_async_copy(rw_hbm, rw_ref, sems.at[2 * CHUNKS + 1]))
    for copy in copies:
        copy.start()
    for c in range(CHUNKS):
        copies[2 * c].wait()
        copies[2 * c + 1].wait()
        for h in range(c * chunk // HEAD_DIM, (c + 1) * chunk // HEAD_DIM):
            cols = slice(h * HEAD_DIM, (h + 1) * HEAD_DIM)
            state_ref[cols, :] = dot(k_ref[:, cols], v_ref[:, cols], ((0,), (0,))).astype(bf16)
    copies[-2].wait()
    copies[-1].wait()
    group, place, core = lax.div(at_ref[0], half), lax.rem(at_ref[0], half), at_ref[1]
    ids = ids_ref[...]
    shares = rw_ref[...] / jnp.sum(rw_ref[...], axis=0, keepdims=True)
    zero = jnp.zeros((PAD - 8, ids.shape[1]), f32)

    def share_of(expert):
        return jnp.sum(jnp.where(ids == expert, shares, 0.0), axis=0, keepdims=True)

    for r, send_ref in enumerate(sends):
        to = lax.rem(place + r, half)
        send_ref[:part, :] = state_ref[pl.ds(pl.multiple_of(to * part, part), part), :]
        rows = []
        for side in (group, 1 - group):
            first = 2 * (side * half + to)
            both = jnp.concatenate([share_of(first + core), share_of(first + 1 - core)], axis=0)
            high = both.astype(bf16).astype(f32)
            rows += [high, both - high]
        send_ref[part:, :] = jnp.concatenate(rows + [zero], axis=0).astype(bf16)


def total_kernel(half, *refs):
    gots, send_ref = refs[:half], refs[half]
    part = gots[0].shape[0] - PAD
    total = gots[0][:part, :].astype(f32)
    for r in range(1, half):
        total = total + gots[r][:part, :].astype(f32)
    send_ref[:part, :] = total.astype(bf16)
    for r in range(half):
        send_ref[part + r * PAD : part + (r + 1) * PAD, :] = gots[r][part:, :]


def prefix_kernel(half, at_ref, far_ref, *refs):
    gots, backs, shares_ref = refs[:half], refs[half:-1], refs[-1]
    part = backs[0].shape[0]
    group, place = lax.div(at_ref[0], half), lax.rem(at_ref[0], half)
    before = jnp.where(group == 1, far_ref[:part, :].astype(f32), 0.0)
    total = before
    for r in range(half):
        total = total + jnp.where(r <= place, gots[r][:part, :].astype(f32), 0.0)
    for r in reversed(range(half)):
        total = jnp.where(r == place, before, total)
        backs[r][...] = total.astype(bf16)
        total = total + gots[r][:part, :].astype(f32)
        source = lax.rem(place + half - r, half)
        terms = gots[r][part:, :].astype(f32)
        shares_ref[group * half + source] = terms[0:8] + terms[2:10]
        terms = far_ref[part + r * PAD : part + (r + 1) * PAD, :].astype(f32)
        shares_ref[(1 - group) * half + source] = terms[4:12] + terms[6:14]


def attention_kernel(half, at_ref, q_ref, k_ref, v_ref, hg_ref, fg_ref, *refs):
    carried, (att_ref, normed_ref, p_ref) = refs[:half], refs[half:]
    rows, width = q_ref.shape
    part = width // half
    for r in range(half):
        s = lax.rem(lax.rem(at_ref[0], half) + r, half)
        p_ref[pl.ds(pl.multiple_of(s * part, part), part), :] = carried[r][...]
    causal = lax.broadcasted_iota(jnp.int32, (rows, rows), 0) >= lax.broadcasted_iota(
        jnp.int32, (rows, rows), 1
    )
    feature_sq = jnp.zeros((rows, HEAD_DIM), f32)
    for h in range(width // HEAD_DIM):
        cols = slice(h * HEAD_DIM, (h + 1) * HEAD_DIM)
        q, v = q_ref[:, cols], v_ref[:, cols]
        scores = jnp.where(causal, dot(q, k_ref[:, cols], ((1,), (1,))), 0.0)
        high = scores.astype(bf16)
        low = (scores - high.astype(f32)).astype(bf16)
        raw = dot(high, v) + dot(low, v) + dot(q, p_ref[cols, :])
        mean_square = jnp.mean(raw * raw, axis=-1, keepdims=True)
        att = (raw * lax.rsqrt(mean_square + epsilon) * hg_ref[:, cols]).astype(bf16)
        att_ref[:, cols] = att
        att = att.astype(f32)
        feature_sq = feature_sq + att * att
    scale = lax.rsqrt(jnp.sum(feature_sq, axis=-1, keepdims=True) / width + epsilon)
    for h in range(width // HEAD_DIM):
        cols = slice(h * HEAD_DIM, (h + 1) * HEAD_DIM)
        normed_ref[:, cols] = (att_ref[:, cols].astype(f32) * scale * fg_ref[:, cols]).astype(bf16)


def expert_kernel(hop, at_ref, x_ref, w_ref, g0, u0, d0, g1, u1, d1, out_ref):
    n_seq = w_ref.shape[0]
    seq, core = at_ref[0], at_ref[1]
    last = n_seq - 1
    place = jnp.where(seq % 2 == 0, seq // 2, last - seq // 2)
    place = lax.rem(place + jnp.where(core == 0, n_seq - hop, hop), n_seq)
    source = jnp.where(2 * place < n_seq, 2 * place, 2 * (last - place) + 1)
    shares = jnp.transpose(w_ref[source])
    x = x_ref[...]
    total = None
    for e, (g, u, d) in enumerate(((g0, u0, d0), (g1, u1, d1))):
        gate = dot(x, g[...])
        up = dot(x, u[...])
        hidden = (gate / (1.0 + jnp.exp(-gate)) * up * shares[:, e : e + 1]).astype(bf16)
        part = dot(hidden, d[...])
        total = part if total is None else total + part
    out_ref[...] = total.astype(bf16)


def run_experts(hop, at, x, shares, weights):
    rows, width = x.shape
    hidden = weights[0].shape[1]
    return pl.pallas_call(
        functools.partial(expert_kernel, hop),
        in_specs=[SMEM] + [VMEM] * 8,
        out_specs=VMEM,
        out_shape=jax.ShapeDtypeStruct((rows, width), bf16),
        compiler_params=pltpu.CompilerParams(vmem_limit_bytes=24 << 20),
        cost_estimate=pl.CostEstimate(
            flops=12 * rows * width * hidden,
            bytes_accessed=4 * rows * width,
            transcendentals=2 * rows * hidden,
        ),
        name="experts",
    )(at, x, shares, *weights)


def in_hbm(*arrays):
    return [pltpu.with_memory_space_constraint(a, pltpu.HBM) for a in arrays]


def load_kernel(count, after_ref, *refs):
    del after_ref
    sems = refs[-1]
    copies = [pltpu.make_async_copy(refs[i], refs[count + i], sems.at[i]) for i in range(count)]
    for copy in copies:
        copy.start()
    for copy in copies:
        copy.wait()


def load(after, *arrays):
    arrays = in_hbm(*arrays)
    count = len(arrays)
    size = sum(a.size * a.dtype.itemsize for a in arrays)
    return pl.pallas_call(
        functools.partial(load_kernel, count),
        in_specs=[HBM] * (count + 1),
        out_specs=[VMEM] * count,
        out_shape=[jax.ShapeDtypeStruct(a.shape, a.dtype) for a in arrays],
        scratch_shapes=[pltpu.SemaphoreType.DMA((count,))],
        compiler_params=pltpu.CompilerParams(vmem_limit_bytes=1 << 20),
        cost_estimate=pl.CostEstimate(flops=0, bytes_accessed=size, transcendentals=0),
        name="load",
    )(after, *arrays)


def ring_of(n_seq):
    return list(range(0, n_seq, 2)) + list(range(n_seq - 1, 0, -2)) if n_seq > 1 else [0]


def per_device(
    n_seq,
    queries,
    key_rows,
    value_rows,
    head_gain,
    ffn_gain,
    expert_ids,
    router_weight,
    w_gate,
    w_up,
    w_down,
):
    _, rows, width = queries.shape
    q, k, v = queries[0], key_rows[0], value_rows[0]
    own = (w_gate[0], w_up[0], w_down[0])
    other = tuple(lax.ppermute(w, "expert", [(0, 1), (1, 0)]) for w in own)
    half = n_seq // 2
    at = jnp.stack([lax.axis_index("seq"), lax.axis_index("expert")])

    ring = ring_of(n_seq)
    hops = []
    for i, s in enumerate(ring):
        hops.append((2 * s, 2 * ring[(i + 1) % n_seq]))
        hops.append((2 * s + 1, 2 * ring[i - 1] + 1))

    def hop(value):
        return lax.ppermute(value, ("seq", "expert"), hops)

    def along(blocks, sign):
        def to(s, r):
            return s // half * half + (s + sign * r) % half

        return [blocks[0]] + [
            lax.ppermute(blocks[r], "seq", [(s, to(s, r)) for s in range(n_seq)])
            for r in range(1, half)
        ]

    part = width // half
    sends = pl.pallas_call(
        functools.partial(state_kernel, half),
        in_specs=[SMEM] + [HBM] * 4,
        out_specs=[VMEM] * half,
        scratch_shapes=[
            pltpu.VMEM((width, HEAD_DIM), bf16),
            pltpu.VMEM(expert_ids.shape[:0:-1], jnp.int32),
            pltpu.VMEM(expert_ids.shape[:0:-1], f32),
            pltpu.VMEM((rows, width), bf16),
            pltpu.VMEM((rows, width), bf16),
            pltpu.SemaphoreType.DMA((2 * CHUNKS + 2,)),
        ],
        compiler_params=SMALL,
        out_shape=[jax.ShapeDtypeStruct((part + PAD, HEAD_DIM), bf16)] * half,
        name="states",
    )(at, *in_hbm(expert_ids[0].T, router_weight[0].T, k, v))
    arrays = load(sends[0], q, k, v, head_gain.reshape(1, width), ffn_gain.reshape(1, width))
    gots = along(sends, 1)
    near = pl.pallas_call(
        functools.partial(total_kernel, half),
        in_specs=[VMEM] * half,
        out_specs=VMEM,
        compiler_params=SMALL,
        out_shape=jax.ShapeDtypeStruct((part + PAD * half, HEAD_DIM), bf16),
        name="total",
    )(*gots)
    far = lax.ppermute(near, "seq", [(s, (s + half) % n_seq) for s in range(n_seq)])
    *backs, shares = pl.pallas_call(
        functools.partial(prefix_kernel, half),
        in_specs=[SMEM] + [VMEM] * (half + 1),
        out_specs=[VMEM] * (half + 1),
        compiler_params=SMALL,
        out_shape=[jax.ShapeDtypeStruct((part, HEAD_DIM), bf16)] * half
        + [jax.ShapeDtypeStruct((n_seq, 8, rows), f32)],
        name="prefix",
    )(at, far, *gots)
    attention, normed = pl.pallas_call(
        functools.partial(attention_kernel, half),
        in_specs=[SMEM] + [VMEM] * (half + 5),
        out_specs=[VMEM] * 2,
        scratch_shapes=[pltpu.VMEM((width, HEAD_DIM), bf16)],
        compiler_params=SMALL,
        out_shape=[jax.ShapeDtypeStruct((rows, width), bf16)] * 2,
        name="attend",
    )(at, *arrays, *along(backs, -1))
    weights = load(normed, *own, *other)

    held, partial, first = normed, None, None
    for step in range(n_seq):
        following = hop(held) if step < n_seq - 1 else held
        if step == 0:
            following, *weights = lax.optimization_barrier((following, *weights))
        result = run_experts(step, at, held, shares, weights)
        if step == 0:
            first = result
        elif step == 1:
            partial = result
        else:
            partial = (hop(partial).astype(f32) + result.astype(f32)).astype(bf16)
        held = following
    if n_seq > 1:
        mixture = hop(partial).astype(f32) + first.astype(f32)
    else:
        mixture = first.astype(f32)
    layer_out = (attention.astype(f32) + mixture).astype(bf16)
    return attention[None], layer_out[None]


def solution(mesh):
    tokens = P(("groups", "expert"), "seq", None)
    experts = P(("seq", "expert"), None, None)
    return jax.shard_map(
        functools.partial(per_device, mesh.shape["seq"]),
        mesh=mesh,
        in_specs=(tokens, tokens, tokens, P(), P(), tokens, tokens, experts, experts, experts),
        out_specs=(tokens, tokens),
        check_vma=False,
    )
```

```python
import functools

import jax
import jax.numpy as jnp
from jax import lax
from jax.experimental import pallas as pl
from jax.experimental.pallas import tpu as pltpu
from jax.sharding import PartitionSpec as P


HEAD_DIM = 128
PAD = 16
CHUNKS = 4
PIECES = 2

epsilon = 1e-06
f32 = jnp.float32
bf16 = jnp.bfloat16


VMEM = pl.BlockSpec(memory_space=pltpu.VMEM)
ANY = pl.BlockSpec(memory_space=pl.ANY)
HBM = pl.BlockSpec(memory_space=pltpu.HBM)
SMEM = pl.BlockSpec(memory_space=pltpu.SMEM)
SMALL = pltpu.CompilerParams(vmem_limit_bytes=16 << 20)


def dot(a, b, dims=((1,), (0,))):
    return lax.dot_general(a, b, (dims, ((), ())), preferred_element_type=f32)


def state_kernel(half, at_ref, ids_hbm, rw_hbm, k_hbm, v_hbm, *refs):
    sends, (state_ref, ids_ref, rw_ref, k_ref, v_ref, sems) = refs[:half], refs[half:]
    width = k_ref.shape[1]
    part = width // half
    chunk = width // CHUNKS
    copies = []
    for c in range(CHUNKS):
        cols = slice(c * chunk, (c + 1) * chunk)
        for i, (src, dst) in enumerate(((k_hbm, k_ref), (v_hbm, v_ref))):
            copies.append(pltpu.make_async_copy(src.at[:, cols], dst.at[:, cols], sems.at[2 * c + i]))
    copies.append(pltpu.make_async_copy(ids_hbm, ids_ref, sems.at[2 * CHUNKS]))
    copies.append(pltpu.make_async_copy(rw_hbm, rw_ref, sems.at[2 * CHUNKS + 1]))
    for copy in copies:
        copy.start()
    for c in range(CHUNKS):
        copies[2 * c].wait()
        copies[2 * c + 1].wait()
        for h in range(c * chunk // HEAD_DIM, (c + 1) * chunk // HEAD_DIM):
            cols = slice(h * HEAD_DIM, (h + 1) * HEAD_DIM)
            state_ref[cols, :] = dot(k_ref[:, cols], v_ref[:, cols], ((0,), (0,))).astype(bf16)
    copies[-2].wait()
    copies[-1].wait()
    group, place, core = lax.div(at_ref[0], half), lax.rem(at_ref[0], half), at_ref[1]
    ids = ids_ref[...]
    shares = rw_ref[...] / jnp.sum(rw_ref[...], axis=0, keepdims=True)
    zero = jnp.zeros((PAD - 8, ids.shape[1]), f32)

    def share_of(expert):
        return jnp.sum(jnp.where(ids == expert, shares, 0.0), axis=0, keepdims=True)

    for r, send_ref in enumerate(sends):
        to = lax.rem(place + r, half)
        send_ref[:part, :] = state_ref[pl.ds(pl.multiple_of(to * part, part), part), :]
        rows = []
        for side in (group, 1 - group):
            first = 2 * (side * half + to)
            both = jnp.concatenate([share_of(first + core), share_of(first + 1 - core)], axis=0)
            high = both.astype(bf16).astype(f32)
            rows += [high, both - high]
        send_ref[part:, :] = jnp.concatenate(rows + [zero], axis=0).astype(bf16)


def total_kernel(half, *refs):
    gots, send_ref = refs[:half], refs[half]
    part = gots[0].shape[0] - PAD
    total = gots[0][:part, :].astype(f32)
    for r in range(1, half):
        total = total + gots[r][:part, :].astype(f32)
    send_ref[:part, :] = total.astype(bf16)
    for r in range(half):
        send_ref[part + r * PAD : part + (r + 1) * PAD, :] = gots[r][part:, :]


def prefix_kernel(half, at_ref, after_ref, far_ref, *refs):
    del after_ref
    gots, backs, shares_ref = refs[:half], refs[half:-1], refs[-1]
    part = backs[0].shape[0]
    group, place = lax.div(at_ref[0], half), lax.rem(at_ref[0], half)
    before = jnp.where(group == 1, far_ref[:part, :].astype(f32), 0.0)
    total = before
    for r in range(half):
        total = total + jnp.where(r <= place, gots[r][:part, :].astype(f32), 0.0)
    for r in reversed(range(half)):
        total = jnp.where(r == place, before, total)
        backs[r][...] = total.astype(bf16)
        total = total + gots[r][:part, :].astype(f32)
        source = lax.rem(place + half - r, half)
        terms = gots[r][part:, :].astype(f32)
        shares_ref[group * half + source] = terms[0:8] + terms[2:10]
        terms = far_ref[part + r * PAD : part + (r + 1) * PAD, :].astype(f32)
        shares_ref[(1 - group) * half + source] = terms[4:12] + terms[6:14]


def local_kernel(q_ref, k_ref, v_ref, within_ref):
    rows, width = q_ref.shape
    causal = lax.broadcasted_iota(jnp.int32, (rows, rows), 0) >= lax.broadcasted_iota(
        jnp.int32, (rows, rows), 1
    )
    for h in range(width // HEAD_DIM):
        cols = slice(h * HEAD_DIM, (h + 1) * HEAD_DIM)
        v = v_ref[:, cols]
        scores = jnp.where(causal, dot(q_ref[:, cols], k_ref[:, cols], ((1,), (1,))), 0.0)
        high = scores.astype(bf16)
        low = (scores - high.astype(f32)).astype(bf16)
        within_ref[:, cols] = dot(high, v) + dot(low, v)


def attention_kernel(half, first, at_ref, after_ref, q_ref, within_ref, hg_ref, fg_ref, *refs):
    del after_ref
    carried, (att_ref, normed_ref, p_ref) = refs[:half], refs[half:]
    rows, width = att_ref.shape
    take = slice(first, first + rows)
    part = width // half
    for r in range(half):
        s = lax.rem(lax.rem(at_ref[0], half) + r, half)
        p_ref[pl.ds(pl.multiple_of(s * part, part), part), :] = carried[r][...]
    feature_sq = jnp.zeros((rows, HEAD_DIM), f32)
    for h in range(width // HEAD_DIM):
        cols = slice(h * HEAD_DIM, (h + 1) * HEAD_DIM)
        raw = within_ref[take, cols] + dot(q_ref[take, cols], p_ref[cols, :])
        mean_square = jnp.mean(raw * raw, axis=-1, keepdims=True)
        att = (raw * lax.rsqrt(mean_square + epsilon) * hg_ref[:, cols]).astype(bf16)
        att_ref[:, cols] = att
        att = att.astype(f32)
        feature_sq = feature_sq + att * att
    scale = lax.rsqrt(jnp.sum(feature_sq, axis=-1, keepdims=True) / width + epsilon)
    for h in range(width // HEAD_DIM):
        cols = slice(h * HEAD_DIM, (h + 1) * HEAD_DIM)
        normed_ref[:, cols] = (att_ref[:, cols].astype(f32) * scale * fg_ref[:, cols]).astype(bf16)


def expert_kernel(hop, at_ref, w_ref, g0, u0, d0, g1, u1, d1, *refs):
    n_seq = w_ref.shape[0]
    seq, core = at_ref[0], at_ref[1]
    last = n_seq - 1
    place = jnp.where(seq % 2 == 0, seq // 2, last - seq // 2)
    place = lax.rem(place + jnp.where(core == 0, n_seq - hop, hop), n_seq)
    source = jnp.where(2 * place < n_seq, 2 * place, 2 * (last - place) + 1)
    shares = jnp.transpose(w_ref[source])
    parts = len(refs) // 2
    x = jnp.concatenate([ref[...] for ref in refs[:parts]], axis=0)
    total = None
    for e, (g, u, d) in enumerate(((g0, u0, d0), (g1, u1, d1))):
        gate = dot(x, g[...])
        up = dot(x, u[...])
        hidden = (gate / (1.0 + jnp.exp(-gate)) * up * shares[:, e : e + 1]).astype(bf16)
        part = dot(hidden, d[...])
        total = part if total is None else total + part
    rows = total.shape[0] // parts
    for i, out_ref in enumerate(refs[parts:]):
        out_ref[...] = total[i * rows : (i + 1) * rows].astype(bf16)


def run_experts(hop, at, pieces, shares, weights):
    rows, width = pieces[0].shape
    hidden = weights[0].shape[1]
    count = len(pieces)
    return pl.pallas_call(
        functools.partial(expert_kernel, hop),
        in_specs=[SMEM] + [VMEM] * (7 + count),
        out_specs=[VMEM] * count,
        out_shape=[jax.ShapeDtypeStruct((rows, width), bf16)] * count,
        compiler_params=pltpu.CompilerParams(vmem_limit_bytes=24 << 20),
        cost_estimate=pl.CostEstimate(
            flops=12 * count * rows * width * hidden,
            bytes_accessed=4 * count * rows * width,
            transcendentals=2 * count * rows * hidden,
        ),
        name="experts",
    )(at, shares, *weights, *pieces)


def in_hbm(*arrays):
    return [pltpu.with_memory_space_constraint(a, pltpu.HBM) for a in arrays]


def load_kernel(count, after_ref, *refs):
    del after_ref
    sems = refs[-1]
    copies = [pltpu.make_async_copy(refs[i], refs[count + i], sems.at[i]) for i in range(count)]
    for copy in copies:
        copy.start()
    for copy in copies:
        copy.wait()


def load(after, *arrays):
    arrays = in_hbm(*arrays)
    count = len(arrays)
    size = sum(a.size * a.dtype.itemsize for a in arrays)
    return pl.pallas_call(
        functools.partial(load_kernel, count),
        in_specs=[HBM] * (count + 1),
        out_specs=[VMEM] * count,
        out_shape=[jax.ShapeDtypeStruct(a.shape, a.dtype) for a in arrays],
        scratch_shapes=[pltpu.SemaphoreType.DMA((count,))],
        compiler_params=pltpu.CompilerParams(vmem_limit_bytes=1 << 20),
        cost_estimate=pl.CostEstimate(flops=0, bytes_accessed=size, transcendentals=0),
        name="load",
    )(after, *arrays)


def ring_of(n_seq):
    return list(range(0, n_seq, 2)) + list(range(n_seq - 1, 0, -2)) if n_seq > 1 else [0]


def per_device(
    n_seq,
    queries,
    key_rows,
    value_rows,
    head_gain,
    ffn_gain,
    expert_ids,
    router_weight,
    w_gate,
    w_up,
    w_down,
):
    _, rows, width = queries.shape
    q, k, v = queries[0], key_rows[0], value_rows[0]
    own = (w_gate[0], w_up[0], w_down[0])
    other = tuple(lax.ppermute(w, "expert", [(0, 1), (1, 0)]) for w in own)
    half = n_seq // 2
    at = jnp.stack([lax.axis_index("seq"), lax.axis_index("expert")])

    ring = ring_of(n_seq)
    hops = []
    for i, s in enumerate(ring):
        hops.append((2 * s, 2 * ring[(i + 1) % n_seq]))
        hops.append((2 * s + 1, 2 * ring[i - 1] + 1))

    def hop(value):
        return lax.ppermute(value, ("seq", "expert"), hops)

    def along(blocks, sign):
        def to(s, r):
            return s // half * half + (s + sign * r) % half

        return [blocks[0]] + [
            lax.ppermute(blocks[r], "seq", [(s, to(s, r)) for s in range(n_seq)])
            for r in range(1, half)
        ]

    part = width // half
    sends = pl.pallas_call(
        functools.partial(state_kernel, half),
        in_specs=[SMEM] + [HBM] * 4,
        out_specs=[VMEM] * half,
        scratch_shapes=[
            pltpu.VMEM((width, HEAD_DIM), bf16),
            pltpu.VMEM(expert_ids.shape[:0:-1], jnp.int32),
            pltpu.VMEM(expert_ids.shape[:0:-1], f32),
            pltpu.VMEM((rows, width), bf16),
            pltpu.VMEM((rows, width), bf16),
            pltpu.SemaphoreType.DMA((2 * CHUNKS + 2,)),
        ],
        compiler_params=SMALL,
        out_shape=[jax.ShapeDtypeStruct((part + PAD, HEAD_DIM), bf16)] * half,
        name="states",
    )(at, *in_hbm(expert_ids[0].T, router_weight[0].T, k, v))
    q, k, v, head_gain, ffn_gain = load(
        sends[0], q, k, v, head_gain.reshape(1, width), ffn_gain.reshape(1, width)
    )
    within = pl.pallas_call(
        local_kernel,
        in_specs=[VMEM] * 3,
        out_specs=VMEM,
        out_shape=jax.ShapeDtypeStruct((rows, width), f32),
        compiler_params=SMALL,
        cost_estimate=pl.CostEstimate(
            flops=6 * rows * rows * width, bytes_accessed=10 * rows * width, transcendentals=0
        ),
        name="local",
    )(q, k, v)
    gots = along(sends, 1)
    near = pl.pallas_call(
        functools.partial(total_kernel, half),
        in_specs=[VMEM] * half,
        out_specs=VMEM,
        compiler_params=SMALL,
        out_shape=jax.ShapeDtypeStruct((part + PAD * half, HEAD_DIM), bf16),
        name="total",
    )(*gots)
    far = lax.ppermute(near, "seq", [(s, (s + half) % n_seq) for s in range(n_seq)])
    *backs, shares = pl.pallas_call(
        functools.partial(prefix_kernel, half),
        in_specs=[SMEM, ANY] + [VMEM] * (half + 1),
        out_specs=[VMEM] * (half + 1),
        compiler_params=SMALL,
        out_shape=[jax.ShapeDtypeStruct((part, HEAD_DIM), bf16)] * half
        + [jax.ShapeDtypeStruct((n_seq, 8, rows), f32)],
        name="prefix",
    )(at, within, far, *gots)
    carried = along(backs, -1)
    piece = rows // PIECES
    attention, normed = [], []
    for i in range(PIECES):
        att_piece, normed_piece = pl.pallas_call(
            functools.partial(attention_kernel, half, i * piece),
            in_specs=[SMEM, ANY] + [VMEM] * (half + 4),
            out_specs=[VMEM] * 2,
            scratch_shapes=[pltpu.VMEM((width, HEAD_DIM), bf16)],
            compiler_params=SMALL,
            cost_estimate=pl.CostEstimate(
                flops=2 * piece * width * HEAD_DIM,
                bytes_accessed=2 * width * HEAD_DIM + 10 * piece * width,
                transcendentals=0,
            ),
            out_shape=[jax.ShapeDtypeStruct((piece, width), bf16)] * 2,
            name="attend",
        )(at, normed[-1] if normed else within, q, within, head_gain, ffn_gain, *carried)
        attention.append(att_piece)
        normed.append(normed_piece)
    weights = load(normed[-1], *own, *other)

    held, partial, first = normed, None, None
    for step in range(n_seq):
        following = [hop(x) for x in held] if step < n_seq - 1 else held
        if step == 0:
            following[0], *weights = lax.optimization_barrier((following[0], *weights))
        result = run_experts(step, at, held, shares, weights)
        if step == 0:
            first = result
        elif step == 1:
            partial = result
        else:
            partial = [hop(x) for x in partial]
            partial = [(p.astype(f32) + r.astype(f32)).astype(bf16) for p, r in zip(partial, result)]
        held = following
    partial = [hop(x) for x in partial]
    layer_out = [
        (a.astype(f32) + (p.astype(f32) + r.astype(f32))).astype(bf16)
        for a, p, r in zip(attention, partial, first)
    ]
    return jnp.concatenate(attention)[None], jnp.concatenate(layer_out)[None]


def solution(mesh):
    n_seq = mesh.shape["seq"]

    def body(*args):
        return per_device(n_seq, *args)

    tokens = P(("groups", "expert"), "seq", None)
    experts = P(("seq", "expert"), None, None)
    return jax.shard_map(
        body,
        mesh=mesh,
        in_specs=(tokens, tokens, tokens, P(), P(), tokens, tokens, experts, experts, experts),
        out_specs=(tokens, tokens),
        check_vma=False,
    )
```

```python
import functools

import jax
import jax.numpy as jnp
from jax import lax
from jax.experimental import pallas as pl
from jax.experimental.pallas import tpu as pltpu
from jax.sharding import PartitionSpec as P


HEAD_DIM = 128
PAD = 16
CHUNKS = 4
PIECES = 2

epsilon = 1e-06
f32 = jnp.float32
bf16 = jnp.bfloat16


VMEM = pl.BlockSpec(memory_space=pltpu.VMEM)
ANY = pl.BlockSpec(memory_space=pl.ANY)
HBM = pl.BlockSpec(memory_space=pltpu.HBM)
SMEM = pl.BlockSpec(memory_space=pltpu.SMEM)
SMALL = pltpu.CompilerParams(vmem_limit_bytes=16 << 20)


def dot(a, b, dims=((1,), (0,))):
    return lax.dot_general(a, b, (dims, ((), ())), preferred_element_type=f32)


def state_kernel(half, at_ref, ids_hbm, rw_hbm, k_hbm, v_hbm, *refs):
    sends, (state_ref, ids_ref, rw_ref, k_ref, v_ref, sems) = refs[:half], refs[half:]
    width = k_ref.shape[1]
    part = width // half
    chunk = width // CHUNKS
    copies = []
    for c in range(CHUNKS):
        cols = slice(c * chunk, (c + 1) * chunk)
        for i, (src, dst) in enumerate(((k_hbm, k_ref), (v_hbm, v_ref))):
            copies.append(pltpu.make_async_copy(src.at[:, cols], dst.at[:, cols], sems.at[2 * c + i]))
    copies.append(pltpu.make_async_copy(ids_hbm, ids_ref, sems.at[2 * CHUNKS]))
    copies.append(pltpu.make_async_copy(rw_hbm, rw_ref, sems.at[2 * CHUNKS + 1]))
    for copy in copies:
        copy.start()
    for c in range(CHUNKS):
        copies[2 * c].wait()
        copies[2 * c + 1].wait()
        for h in range(c * chunk // HEAD_DIM, (c + 1) * chunk // HEAD_DIM):
            cols = slice(h * HEAD_DIM, (h + 1) * HEAD_DIM)
            state_ref[cols, :] = dot(k_ref[:, cols], v_ref[:, cols], ((0,), (0,))).astype(bf16)
    copies[-2].wait()
    copies[-1].wait()
    group, place, core = lax.div(at_ref[0], half), lax.rem(at_ref[0], half), at_ref[1]
    ids = ids_ref[...]
    shares = rw_ref[...] / jnp.sum(rw_ref[...], axis=0, keepdims=True)
    zero = jnp.zeros((PAD - 8, ids.shape[1]), f32)

    def share_of(expert):
        return jnp.sum(jnp.where(ids == expert, shares, 0.0), axis=0, keepdims=True)

    for r, send_ref in enumerate(sends):
        to = lax.rem(place + r, half)
        send_ref[:part, :] = state_ref[pl.ds(pl.multiple_of(to * part, part), part), :]
        rows = []
        for side in (group, 1 - group):
            first = 2 * (side * half + to)
            both = jnp.concatenate([share_of(first + core), share_of(first + 1 - core)], axis=0)
            high = both.astype(bf16).astype(f32)
            rows += [high, both - high]
        send_ref[part:, :] = jnp.concatenate(rows + [zero], axis=0).astype(bf16)


def total_kernel(half, after_ref, *refs):
    del after_ref
    gots, send_ref = refs[:half], refs[half]
    part = gots[0].shape[0] - PAD
    total = gots[0][:part, :].astype(f32)
    for r in range(1, half):
        total = total + gots[r][:part, :].astype(f32)
    send_ref[:part, :] = total.astype(bf16)
    for r in range(half):
        send_ref[part + r * PAD : part + (r + 1) * PAD, :] = gots[r][part:, :]


def prefix_kernel(half, at_ref, after_ref, far_ref, *refs):
    del after_ref
    gots, backs, shares_ref = refs[:half], refs[half:-1], refs[-1]
    part = backs[0].shape[0]
    group, place = lax.div(at_ref[0], half), lax.rem(at_ref[0], half)
    before = jnp.where(group == 1, far_ref[:part, :].astype(f32), 0.0)
    total = before
    for r in range(half):
        total = total + jnp.where(r <= place, gots[r][:part, :].astype(f32), 0.0)
    for r in reversed(range(half)):
        total = jnp.where(r == place, before, total)
        backs[r][...] = total.astype(bf16)
        total = total + gots[r][:part, :].astype(f32)
        source = lax.rem(place + half - r, half)
        terms = gots[r][part:, :].astype(f32)
        shares_ref[group * half + source] = terms[0:8] + terms[2:10]
        terms = far_ref[part + r * PAD : part + (r + 1) * PAD, :].astype(f32)
        shares_ref[(1 - group) * half + source] = terms[4:12] + terms[6:14]


def local_kernel(q_ref, k_ref, v_ref, within_ref):
    rows, width = q_ref.shape
    causal = lax.broadcasted_iota(jnp.int32, (rows, rows), 0) >= lax.broadcasted_iota(
        jnp.int32, (rows, rows), 1
    )
    for h in range(width // HEAD_DIM):
        cols = slice(h * HEAD_DIM, (h + 1) * HEAD_DIM)
        v = v_ref[:, cols]
        scores = jnp.where(causal, dot(q_ref[:, cols], k_ref[:, cols], ((1,), (1,))), 0.0)
        high = scores.astype(bf16)
        low = (scores - high.astype(f32)).astype(bf16)
        within_ref[:, cols] = dot(high, v) + dot(low, v)


def attention_kernel(half, first, at_ref, after_ref, q_ref, within_ref, hg_ref, fg_ref, *refs):
    del after_ref
    carried, (att_ref, normed_ref, p_ref) = refs[:half], refs[half:]
    rows, width = att_ref.shape
    take = slice(first, first + rows)
    part = width // half
    for r in range(half):
        s = lax.rem(lax.rem(at_ref[0], half) + r, half)
        p_ref[pl.ds(pl.multiple_of(s * part, part), part), :] = carried[r][...]
    feature_sq = jnp.zeros((rows, HEAD_DIM), f32)
    for h in range(width // HEAD_DIM):
        cols = slice(h * HEAD_DIM, (h + 1) * HEAD_DIM)
        raw = within_ref[take, cols] + dot(q_ref[take, cols], p_ref[cols, :])
        mean_square = jnp.mean(raw * raw, axis=-1, keepdims=True)
        att = (raw * lax.rsqrt(mean_square + epsilon) * hg_ref[:, cols]).astype(bf16)
        att_ref[:, cols] = att
        att = att.astype(f32)
        feature_sq = feature_sq + att * att
    scale = lax.rsqrt(jnp.sum(feature_sq, axis=-1, keepdims=True) / width + epsilon)
    for h in range(width // HEAD_DIM):
        cols = slice(h * HEAD_DIM, (h + 1) * HEAD_DIM)
        normed_ref[:, cols] = (att_ref[:, cols].astype(f32) * scale * fg_ref[:, cols]).astype(bf16)


def expert_kernel(hop, at_ref, w_ref, g0, u0, d0, g1, u1, d1, *refs):
    n_seq = w_ref.shape[0]
    seq, core = at_ref[0], at_ref[1]
    last = n_seq - 1
    place = jnp.where(seq % 2 == 0, seq // 2, last - seq // 2)
    place = lax.rem(place + jnp.where(core == 0, n_seq - hop, hop), n_seq)
    source = jnp.where(2 * place < n_seq, 2 * place, 2 * (last - place) + 1)
    shares = jnp.transpose(w_ref[source])
    parts = len(refs) // 2
    x = jnp.concatenate([ref[...] for ref in refs[:parts]], axis=0)
    total = None
    for e, (g, u, d) in enumerate(((g0, u0, d0), (g1, u1, d1))):
        gate = dot(x, g[...])
        up = dot(x, u[...])
        hidden = (gate / (1.0 + jnp.exp(-gate)) * up * shares[:, e : e + 1]).astype(bf16)
        part = dot(hidden, d[...])
        total = part if total is None else total + part
    rows = total.shape[0] // parts
    for i, out_ref in enumerate(refs[parts:]):
        out_ref[...] = total[i * rows : (i + 1) * rows].astype(bf16)


def run_experts(hop, at, pieces, shares, weights):
    rows, width = pieces[0].shape
    hidden = weights[0].shape[1]
    count = len(pieces)
    return pl.pallas_call(
        functools.partial(expert_kernel, hop),
        in_specs=[SMEM] + [VMEM] * (7 + count),
        out_specs=[VMEM] * count,
        out_shape=[jax.ShapeDtypeStruct((rows, width), bf16)] * count,
        compiler_params=pltpu.CompilerParams(vmem_limit_bytes=24 << 20),
        cost_estimate=pl.CostEstimate(
            flops=12 * count * rows * width * hidden,
            bytes_accessed=4 * count * rows * width,
            transcendentals=2 * count * rows * hidden,
        ),
        name="experts",
    )(at, shares, *weights, *pieces)


def in_hbm(*arrays):
    return [pltpu.with_memory_space_constraint(a, pltpu.HBM) for a in arrays]


def load_kernel(count, after_ref, *refs):
    del after_ref
    sems = refs[-1]
    copies = [pltpu.make_async_copy(refs[i], refs[count + i], sems.at[i]) for i in range(count)]
    for copy in copies:
        copy.start()
    for copy in copies:
        copy.wait()


def load(after, *arrays):
    arrays = in_hbm(*arrays)
    count = len(arrays)
    size = sum(a.size * a.dtype.itemsize for a in arrays)
    return pl.pallas_call(
        functools.partial(load_kernel, count),
        in_specs=[HBM] * (count + 1),
        out_specs=[VMEM] * count,
        out_shape=[jax.ShapeDtypeStruct(a.shape, a.dtype) for a in arrays],
        scratch_shapes=[pltpu.SemaphoreType.DMA((count,))],
        compiler_params=pltpu.CompilerParams(vmem_limit_bytes=1 << 20),
        cost_estimate=pl.CostEstimate(flops=0, bytes_accessed=size, transcendentals=0),
        name="load",
    )(after, *arrays)


def ring_of(n_seq):
    return list(range(0, n_seq, 2)) + list(range(n_seq - 1, 0, -2)) if n_seq > 1 else [0]


def per_device(
    n_seq,
    queries,
    key_rows,
    value_rows,
    head_gain,
    ffn_gain,
    expert_ids,
    router_weight,
    w_gate,
    w_up,
    w_down,
):
    _, rows, width = queries.shape
    q, k, v = queries[0], key_rows[0], value_rows[0]
    own = (w_gate[0], w_up[0], w_down[0])
    half = n_seq // 2
    at = jnp.stack([lax.axis_index("seq"), lax.axis_index("expert")])

    ring = ring_of(n_seq)
    hops = []
    for i, s in enumerate(ring):
        hops.append((2 * s, 2 * ring[(i + 1) % n_seq]))
        hops.append((2 * s + 1, 2 * ring[i - 1] + 1))

    def hop(value):
        return lax.ppermute(value, ("seq", "expert"), hops)

    def along(blocks, sign):
        moved = [blocks[0]]
        for r in range(1, half):
            pairs = [(s, s // half * half + (s + sign * r) % half) for s in range(n_seq)]
            moved.append(lax.ppermute(blocks[r], "seq", pairs))
        return moved

    part = width // half
    sends = pl.pallas_call(
        functools.partial(state_kernel, half),
        in_specs=[SMEM] + [HBM] * 4,
        out_specs=[VMEM] * half,
        scratch_shapes=[
            pltpu.VMEM((width, HEAD_DIM), bf16),
            pltpu.VMEM(expert_ids.shape[:0:-1], jnp.int32),
            pltpu.VMEM(expert_ids.shape[:0:-1], f32),
            pltpu.VMEM((rows, width), bf16),
            pltpu.VMEM((rows, width), bf16),
            pltpu.SemaphoreType.DMA((2 * CHUNKS + 2,)),
        ],
        compiler_params=SMALL,
        out_shape=[jax.ShapeDtypeStruct((part + PAD, HEAD_DIM), bf16)] * half,
        name="states",
    )(at, *in_hbm(expert_ids[0].T, router_weight[0].T, k, v))
    q, k, v, head_gain, ffn_gain = load(
        sends[0], q, k, v, head_gain.reshape(1, width), ffn_gain.reshape(1, width)
    )
    within = pl.pallas_call(
        local_kernel,
        in_specs=[VMEM] * 3,
        out_specs=VMEM,
        out_shape=jax.ShapeDtypeStruct((rows, width), f32),
        compiler_params=SMALL,
        cost_estimate=pl.CostEstimate(
            flops=6 * rows * rows * width, bytes_accessed=10 * rows * width, transcendentals=0
        ),
        name="local",
    )(q, k, v)
    own = load(sends[0], *own)
    other = [lax.ppermute(w, "expert", [(0, 1), (1, 0)]) for w in own]
    gots = along(sends, 1)
    near = pl.pallas_call(
        functools.partial(total_kernel, half),
        in_specs=[ANY] + [VMEM] * half,
        out_specs=VMEM,
        compiler_params=SMALL,
        out_shape=jax.ShapeDtypeStruct((part + PAD * half, HEAD_DIM), bf16),
        name="total",
    )(own[0], *gots)
    far = lax.ppermute(near, "seq", [(s, (s + half) % n_seq) for s in range(n_seq)])
    *backs, shares = pl.pallas_call(
        functools.partial(prefix_kernel, half),
        in_specs=[SMEM, ANY] + [VMEM] * (half + 1),
        out_specs=[VMEM] * (half + 1),
        compiler_params=SMALL,
        out_shape=[jax.ShapeDtypeStruct((part, HEAD_DIM), bf16)] * half
        + [jax.ShapeDtypeStruct((n_seq, 8, rows), f32)],
        name="prefix",
    )(at, within, far, *gots)
    carried = along(backs, -1)
    piece = rows // PIECES
    attention, normed = [], []
    for i in range(PIECES):
        att_piece, normed_piece = pl.pallas_call(
            functools.partial(attention_kernel, half, i * piece),
            in_specs=[SMEM, ANY] + [VMEM] * (half + 4),
            out_specs=[VMEM] * 2,
            scratch_shapes=[pltpu.VMEM((width, HEAD_DIM), bf16)],
            compiler_params=SMALL,
            cost_estimate=pl.CostEstimate(
                flops=2 * piece * width * HEAD_DIM,
                bytes_accessed=2 * width * HEAD_DIM + 10 * piece * width,
                transcendentals=0,
            ),
            out_shape=[jax.ShapeDtypeStruct((piece, width), bf16)] * 2,
            name="attend",
        )(at, normed[-1] if normed else within, q, within, head_gain, ffn_gain, *carried)
        attention.append(att_piece)
        normed.append(normed_piece)
    weights = [*own, *other]

    held, partial, first = normed, None, None
    for step in range(n_seq):
        following = [hop(x) for x in held] if step < n_seq - 1 else held
        result = run_experts(step, at, held, shares, weights)
        if step == 0:
            first = result
        elif step == 1:
            partial = result
        else:
            partial = [hop(x) for x in partial]
            partial = [(p.astype(f32) + r.astype(f32)).astype(bf16) for p, r in zip(partial, result)]
        held = following
    partial = [hop(x) for x in partial]
    layer_out = [
        (a.astype(f32) + (p.astype(f32) + r.astype(f32))).astype(bf16)
        for a, p, r in zip(attention, partial, first)
    ]
    attention = jnp.concatenate(attention)[None]
    return attention, jnp.concatenate(layer_out)[None]


def solution(mesh):
    n_seq = mesh.shape["seq"]

    def body(*args):
        return per_device(n_seq, *args)

    tokens = P(("groups", "expert"), "seq", None)
    experts = P(("seq", "expert"), None, None)
    return jax.shard_map(
        body,
        mesh=mesh,
        in_specs=(tokens, tokens, tokens, P(), P(), tokens, tokens, experts, experts, experts),
        out_specs=(tokens, tokens),
        check_vma=False,
    )
```

```python
import functools

import jax
import jax.numpy as jnp
from jax import lax
from jax.experimental import pallas as pl
from jax.experimental.pallas import tpu as pltpu
from jax.sharding import PartitionSpec as P


HEAD_DIM = 128
PAD = 16
CHUNKS = 4
PIECES = 2
STRIP = 32

epsilon = 1e-06
f32 = jnp.float32
bf16 = jnp.bfloat16


VMEM = pl.BlockSpec(memory_space=pltpu.VMEM)
ANY = pl.BlockSpec(memory_space=pl.ANY)
HBM = pl.BlockSpec(memory_space=pltpu.HBM)
SMALL = pltpu.CompilerParams(vmem_limit_bytes=16 << 20)


def dot(a, b, dims=((1,), (0,))):
    return lax.dot_general(a, b, (dims, ((), ())), preferred_element_type=f32)


def state_kernel(half, ids_hbm, rw_hbm, k_hbm, v_hbm, *refs):
    sends, (state_ref, ids_ref, rw_ref, k_ref, v_ref, sems) = refs[:half], refs[half:]
    width = k_ref.shape[1]
    part = width // half
    chunk = width // CHUNKS
    copies = []
    for c in range(CHUNKS):
        cols = slice(c * chunk, (c + 1) * chunk)
        for i, (src, dst) in enumerate(((k_hbm, k_ref), (v_hbm, v_ref))):
            copies.append(pltpu.make_async_copy(src.at[:, cols], dst.at[:, cols], sems.at[2 * c + i]))
    copies.append(pltpu.make_async_copy(ids_hbm, ids_ref, sems.at[2 * CHUNKS]))
    copies.append(pltpu.make_async_copy(rw_hbm, rw_ref, sems.at[2 * CHUNKS + 1]))
    for copy in copies[-2:] + copies[:-2]:
        copy.start()
    copies[-2].wait()
    copies[-1].wait()
    group, place, core = lax.div(lax.axis_index("seq"), half), lax.rem(lax.axis_index("seq"), half), lax.axis_index("expert")
    ids = ids_ref[...]
    shares = rw_ref[...] / jnp.sum(rw_ref[...], axis=0, keepdims=True)
    zero = jnp.zeros((PAD - 8, ids.shape[1]), f32)

    def share_of(expert):
        return jnp.sum(jnp.where(ids == expert, shares, 0.0), axis=0, keepdims=True)

    for r, send_ref in enumerate(sends):
        to = lax.rem(place + r, half)
        rows = []
        for side in (group, 1 - group):
            first = 2 * (side * half + to)
            both = jnp.concatenate([share_of(first + core), share_of(first + 1 - core)], axis=0)
            high = both.astype(bf16).astype(f32)
            rows += [high, both - high]
        send_ref[part:, :] = jnp.concatenate(rows + [zero], axis=0).astype(bf16)
    for c in range(CHUNKS):
        copies[2 * c].wait()
        copies[2 * c + 1].wait()
        for h in range(c * chunk // HEAD_DIM, (c + 1) * chunk // HEAD_DIM):
            cols = slice(h * HEAD_DIM, (h + 1) * HEAD_DIM)
            state_ref[cols, :] = dot(k_ref[:, cols], v_ref[:, cols], ((0,), (0,))).astype(bf16)
    for r, send_ref in enumerate(sends):
        to = lax.rem(place + r, half)
        send_ref[:part, :] = state_ref[pl.ds(pl.multiple_of(to * part, part), part), :]


def total_kernel(half, after_ref, *refs):
    del after_ref
    gots, send_ref = refs[:half], refs[half]
    part = gots[0].shape[0] - PAD
    total = gots[0][:part, :].astype(f32)
    for r in range(1, half):
        total = total + gots[r][:part, :].astype(f32)
    send_ref[:part, :] = total.astype(bf16)
    terms = [got_ref[part:, :].astype(f32)[4:8] for got_ref in gots]
    send_ref[part:, :] = jnp.concatenate(terms, axis=0).astype(bf16)


def prefix_kernel(half, after_ref, far_ref, *refs):
    del after_ref
    gots, backs = refs[:half], refs[half:]
    part = backs[0].shape[0]
    group, place = lax.div(lax.axis_index("seq"), half), lax.rem(lax.axis_index("seq"), half)
    for row in range(0, part, STRIP):
        strip = slice(row, row + STRIP)
        states = [got_ref[strip, :].astype(f32) for got_ref in gots]
        before = jnp.where(group == 1, far_ref[strip, :].astype(f32), 0.0)
        total = before
        for r in range(half):
            total = total + jnp.where(r <= place, states[r], 0.0)
        for r in reversed(range(half)):
            total = jnp.where(r == place, before, total)
            backs[r][strip, :] = total.astype(bf16)
            total = total + states[r]


def shares_kernel(half, far_ref, *refs):
    gots, shares_ref = refs[:half], refs[half]
    part = gots[0].shape[0] - PAD
    group, place = lax.div(lax.axis_index("seq"), half), lax.rem(lax.axis_index("seq"), half)
    far = far_ref[part:, :].astype(f32)
    for r in range(half):
        source = lax.rem(place + half - r, half)
        terms = gots[r][part:, :].astype(f32)
        shares_ref[group * half + source, 0:2, :] = terms[0:2] + terms[2:4]
        terms = far[4 * r : 4 * r + 4]
        shares_ref[(1 - group) * half + source, 0:2, :] = terms[0:2] + terms[2:4]


def local_kernel(q_ref, k_ref, v_ref, within_ref):
    rows, width = q_ref.shape
    causal = lax.broadcasted_iota(jnp.int32, (rows, rows), 0) >= lax.broadcasted_iota(
        jnp.int32, (rows, rows), 1
    )
    for h in range(width // HEAD_DIM):
        cols = slice(h * HEAD_DIM, (h + 1) * HEAD_DIM)
        v = v_ref[:, cols]
        scores = jnp.where(causal, dot(q_ref[:, cols], k_ref[:, cols], ((1,), (1,))), 0.0)
        high = scores.astype(bf16)
        low = (scores - high.astype(f32)).astype(bf16)
        within_ref[:, cols] = dot(high, v) + dot(low, v)


def attention_kernel(half, first, after_ref, q_ref, within_ref, hg_ref, fg_ref, *refs):
    del after_ref
    carried, (att_ref, normed_ref) = refs[:half], refs[half:]
    rows, width = att_ref.shape
    take = slice(first, first + rows)
    part = width // half
    feature_sq = jnp.zeros((rows, HEAD_DIM), f32)
    for r in range(half):
        part_of = lax.rem(lax.rem(lax.axis_index("seq"), half) + r, half)
        for h in range(0, part, HEAD_DIM):
            cols = pl.ds(pl.multiple_of(part_of * part + h, HEAD_DIM), HEAD_DIM)
            raw = within_ref[take, cols] + dot(q_ref[take, cols], carried[r][h : h + HEAD_DIM, :])
            mean_square = jnp.mean(raw * raw, axis=-1, keepdims=True)
            att = (raw * lax.rsqrt(mean_square + epsilon) * hg_ref[:, cols]).astype(bf16)
            att_ref[:, cols] = att
            att = att.astype(f32)
            feature_sq = feature_sq + att * att
    scale = lax.rsqrt(jnp.sum(feature_sq, axis=-1, keepdims=True) / width + epsilon)
    for h in range(width // HEAD_DIM):
        cols = slice(h * HEAD_DIM, (h + 1) * HEAD_DIM)
        normed_ref[:, cols] = (att_ref[:, cols].astype(f32) * scale * fg_ref[:, cols]).astype(bf16)


def expert_kernel(hop, w_ref, g0, u0, d0, g1, u1, d1, *refs):
    n_seq = w_ref.shape[0]
    seq, core = lax.axis_index("seq"), lax.axis_index("expert")
    last = n_seq - 1
    place = jnp.where(seq % 2 == 0, seq // 2, last - seq // 2)
    place = lax.rem(place + jnp.where(core == 0, n_seq - hop, hop), n_seq)
    source = jnp.where(2 * place < n_seq, 2 * place, 2 * (last - place) + 1)
    shares = jnp.transpose(w_ref[source])
    parts = len(refs) // 2
    x = jnp.concatenate([ref[...] for ref in refs[:parts]], axis=0)
    total = None
    for e, (g, u, d) in enumerate(((g0, u0, d0), (g1, u1, d1))):
        gate = dot(x, g[...])
        up = dot(x, u[...])
        hidden = (gate / (1.0 + jnp.exp(-gate)) * up * shares[:, e : e + 1]).astype(bf16)
        part = dot(hidden, d[...])
        total = part if total is None else total + part
    rows = total.shape[0] // parts
    for i, out_ref in enumerate(refs[parts:]):
        out_ref[...] = total[i * rows : (i + 1) * rows].astype(bf16)


def run_experts(hop, pieces, shares, weights):
    rows, width = pieces[0].shape
    hidden = weights[0].shape[1]
    count = len(pieces)
    return pl.pallas_call(
        functools.partial(expert_kernel, hop),
        in_specs=[VMEM] * (7 + count),
        out_specs=[VMEM] * count,
        out_shape=[jax.ShapeDtypeStruct((rows, width), bf16)] * count,
        compiler_params=pltpu.CompilerParams(vmem_limit_bytes=24 << 20),
        cost_estimate=pl.CostEstimate(
            flops=12 * count * rows * width * hidden,
            bytes_accessed=4 * count * rows * width,
            transcendentals=2 * count * rows * hidden,
        ),
        name="experts",
    )(shares, *weights, *pieces)


def in_hbm(*arrays):
    return [pltpu.with_memory_space_constraint(a, pltpu.HBM) for a in arrays]


def load_kernel(count, after_ref, *refs):
    del after_ref
    sems = refs[-1]
    copies = [pltpu.make_async_copy(refs[i], refs[count + i], sems.at[i]) for i in range(count)]
    for copy in copies:
        copy.start()
    for copy in copies:
        copy.wait()


def load(after, *arrays):
    arrays = in_hbm(*arrays)
    count = len(arrays)
    size = sum(a.size * a.dtype.itemsize for a in arrays)
    return pl.pallas_call(
        functools.partial(load_kernel, count),
        in_specs=[HBM] * (count + 1),
        out_specs=[VMEM] * count,
        out_shape=[jax.ShapeDtypeStruct(a.shape, a.dtype) for a in arrays],
        scratch_shapes=[pltpu.SemaphoreType.DMA((count,))],
        compiler_params=pltpu.CompilerParams(vmem_limit_bytes=1 << 20),
        cost_estimate=pl.CostEstimate(flops=0, bytes_accessed=size, transcendentals=0),
        name="load",
    )(after, *arrays)


def ring_of(n_seq):
    return list(range(0, n_seq, 2)) + list(range(n_seq - 1, 0, -2)) if n_seq > 1 else [0]


def per_device(
    n_seq,
    queries,
    key_rows,
    value_rows,
    head_gain,
    ffn_gain,
    expert_ids,
    router_weight,
    w_gate,
    w_up,
    w_down,
):
    _, rows, width = queries.shape
    q, k, v = queries[0], key_rows[0], value_rows[0]
    own = (w_gate[0], w_up[0], w_down[0])
    half = n_seq // 2

    ring = ring_of(n_seq)
    hops = []
    for i, s in enumerate(ring):
        hops.append((2 * s, 2 * ring[(i + 1) % n_seq]))
        hops.append((2 * s + 1, 2 * ring[i - 1] + 1))

    def hop(value):
        return lax.ppermute(value, ("seq", "expert"), hops)

    def along(blocks, sign):
        moved = [blocks[0]]
        for r in range(1, half):
            pairs = [(s, s // half * half + (s + sign * r) % half) for s in range(n_seq)]
            moved.append(lax.ppermute(blocks[r], "seq", pairs))
        return moved

    part = width // half
    sends = pl.pallas_call(
        functools.partial(state_kernel, half),
        in_specs=[HBM] * 4,
        out_specs=[VMEM] * half,
        scratch_shapes=[
            pltpu.VMEM((width, HEAD_DIM), bf16),
            pltpu.VMEM(expert_ids.shape[:0:-1], jnp.int32),
            pltpu.VMEM(expert_ids.shape[:0:-1], f32),
            pltpu.VMEM((rows, width), bf16),
            pltpu.VMEM((rows, width), bf16),
            pltpu.SemaphoreType.DMA((2 * CHUNKS + 2,)),
        ],
        compiler_params=SMALL,
        out_shape=[jax.ShapeDtypeStruct((part + PAD, HEAD_DIM), bf16)] * half,
        name="states",
    )(*in_hbm(expert_ids[0].T, router_weight[0].T, k, v))
    q, k, v, head_gain, ffn_gain = load(
        sends[0], q, k, v, head_gain.reshape(1, width), ffn_gain.reshape(1, width)
    )
    within = pl.pallas_call(
        local_kernel,
        in_specs=[VMEM] * 3,
        out_specs=VMEM,
        out_shape=jax.ShapeDtypeStruct((rows, width), f32),
        compiler_params=SMALL,
        cost_estimate=pl.CostEstimate(
            flops=6 * rows * rows * width, bytes_accessed=10 * rows * width, transcendentals=0
        ),
        name="local",
    )(q, k, v)
    own = load(sends[0], *own)
    other = [lax.ppermute(w, "expert", [(0, 1), (1, 0)]) for w in own]
    gots = along(sends, 1)
    near = pl.pallas_call(
        functools.partial(total_kernel, half),
        in_specs=[ANY] + [VMEM] * half,
        out_specs=VMEM,
        compiler_params=SMALL,
        out_shape=jax.ShapeDtypeStruct((part + 4 * half, HEAD_DIM), bf16),
        name="total",
    )(own[0], *gots)
    far = lax.ppermute(near, "seq", [(s, (s + half) % n_seq) for s in range(n_seq)])
    backs = pl.pallas_call(
        functools.partial(prefix_kernel, half),
        in_specs=[ANY] + [VMEM] * (half + 1),
        out_specs=[VMEM] * half,
        compiler_params=SMALL,
        out_shape=[jax.ShapeDtypeStruct((part, HEAD_DIM), bf16)] * half,
        name="prefix",
    )(within, far, *gots)
    shares = pl.pallas_call(
        functools.partial(shares_kernel, half),
        in_specs=[VMEM] * (half + 1),
        out_specs=VMEM,
        compiler_params=SMALL,
        out_shape=jax.ShapeDtypeStruct((n_seq, 8, rows), f32),
        name="shares",
    )(far, *gots)
    carried = along(backs, -1)
    piece = rows // PIECES
    attention, normed = [], []
    for i in range(PIECES):
        att_piece, normed_piece = pl.pallas_call(
            functools.partial(attention_kernel, half, i * piece),
            in_specs=[ANY] + [VMEM] * (half + 4),
            out_specs=[VMEM] * 2,
            compiler_params=SMALL,
            cost_estimate=pl.CostEstimate(
                flops=2 * piece * width * HEAD_DIM,
                bytes_accessed=2 * width * HEAD_DIM + 10 * piece * width,
                transcendentals=0,
            ),
            out_shape=[jax.ShapeDtypeStruct((piece, width), bf16)] * 2,
            name="attend",
        )(normed[-1] if normed else within, q, within, head_gain, ffn_gain, *carried)
        attention.append(att_piece)
        normed.append(normed_piece)
    weights = [*own, *other]

    held, partial, first = normed, None, None
    for step in range(n_seq):
        following = [hop(x) for x in held] if step < n_seq - 1 else held
        result = run_experts(step, held, shares, weights)
        if step == 0:
            first = result
        elif step == 1:
            partial = result
        else:
            partial = [hop(x) for x in partial]
            partial = [(p.astype(f32) + r.astype(f32)).astype(bf16) for p, r in zip(partial, result)]
        held = following
    partial = [hop(x) for x in partial]
    layer_out = [
        (a.astype(f32) + (p.astype(f32) + r.astype(f32))).astype(bf16)
        for a, p, r in zip(attention, partial, first)
    ]
    attention = jnp.concatenate(attention)[None]
    return attention, jnp.concatenate(layer_out)[None]


def solution(mesh):
    n_seq = mesh.shape["seq"]

    def body(*args):
        return per_device(n_seq, *args)

    tokens = P(("groups", "expert"), "seq", None)
    experts = P(("seq", "expert"), None, None)
    return jax.shard_map(
        body,
        mesh=mesh,
        in_specs=(tokens, tokens, tokens, P(), P(), tokens, tokens, experts, experts, experts),
        out_specs=(tokens, tokens),
        check_vma=False,
    )
```

```python
import functools

import jax
import jax.numpy as jnp
from jax import lax
from jax.experimental import pallas as pl
from jax.experimental.pallas import tpu as pltpu
from jax.sharding import PartitionSpec as P


HEAD_DIM = 128
PAD = 16
CHUNKS = 1
PIECES = 2
STRIP = 32

epsilon = 1e-06
f32 = jnp.float32
bf16 = jnp.bfloat16


VMEM = pl.BlockSpec(memory_space=pltpu.VMEM)
ANY = pl.BlockSpec(memory_space=pl.ANY)
HBM = pl.BlockSpec(memory_space=pltpu.HBM)
SMALL = pltpu.CompilerParams(vmem_limit_bytes=16 << 20)


def dot(a, b, dims=((1,), (0,))):
    return lax.dot_general(a, b, (dims, ((), ())), preferred_element_type=f32)


def state_kernel(half, ids_hbm, rw_hbm, k_hbm, v_hbm, *refs):
    sends, (state_ref, ids_ref, rw_ref, k_ref, v_ref, sems) = refs[:half], refs[half:]
    width = k_ref.shape[1]
    part = width // half
    chunk = width // CHUNKS
    copies = []
    for c in range(CHUNKS):
        cols = slice(c * chunk, (c + 1) * chunk)
        for i, (src, dst) in enumerate(((k_hbm, k_ref), (v_hbm, v_ref))):
            copies.append(pltpu.make_async_copy(src.at[:, cols], dst.at[:, cols], sems.at[2 * c + i]))
    copies.append(pltpu.make_async_copy(ids_hbm, ids_ref, sems.at[2 * CHUNKS]))
    copies.append(pltpu.make_async_copy(rw_hbm, rw_ref, sems.at[2 * CHUNKS + 1]))
    for copy in copies[-2:] + copies[:-2]:
        copy.start()
    copies[-2].wait()
    copies[-1].wait()
    group, place, core = lax.div(lax.axis_index("seq"), half), lax.rem(lax.axis_index("seq"), half), lax.axis_index("expert")
    ids = ids_ref[...]
    shares = rw_ref[...] / jnp.sum(rw_ref[...], axis=0, keepdims=True)
    zero = jnp.zeros((PAD - 8, ids.shape[1]), f32)

    def share_of(expert):
        return jnp.sum(jnp.where(ids == expert, shares, 0.0), axis=0, keepdims=True)

    for r, send_ref in enumerate(sends):
        to = lax.bitwise_xor(place, r)
        rows = []
        for side in (group, 1 - group):
            first = 2 * (side * half + to)
            both = jnp.concatenate([share_of(first + core), share_of(first + 1 - core)], axis=0)
            high = both.astype(bf16).astype(f32)
            rows += [high, both - high]
        send_ref[part:, :] = jnp.concatenate(rows + [zero], axis=0).astype(bf16)
    for c in range(CHUNKS):
        copies[2 * c].wait()
        copies[2 * c + 1].wait()
        for h in range(c * chunk // HEAD_DIM, (c + 1) * chunk // HEAD_DIM):
            cols = slice(h * HEAD_DIM, (h + 1) * HEAD_DIM)
            state_ref[cols, :] = dot(k_ref[:, cols], v_ref[:, cols], ((0,), (0,))).astype(bf16)
    for r, send_ref in enumerate(sends):
        to = lax.bitwise_xor(place, r)
        send_ref[:part, :] = state_ref[pl.ds(pl.multiple_of(to * part, part), part), :]


def total_kernel(half, after_ref, *refs):
    del after_ref
    gots, send_ref = refs[:half], refs[half]
    part = gots[0].shape[0] - PAD
    total = gots[0][:part, :].astype(f32)
    for r in range(1, half):
        total = total + gots[r][:part, :].astype(f32)
    send_ref[:part, :] = total.astype(bf16)
    terms = [got_ref[part:, :].astype(f32)[4:8] for got_ref in gots]
    send_ref[part:, :] = jnp.concatenate(terms, axis=0).astype(bf16)


def prefix_kernel(half, after_ref, far_ref, *refs):
    del after_ref
    gots, backs = refs[:half], refs[half:]
    part = backs[0].shape[0]
    group, place = lax.div(lax.axis_index("seq"), half), lax.rem(lax.axis_index("seq"), half)
    sources = [lax.bitwise_xor(place, r) for r in range(half)]
    for row in range(0, part, STRIP):
        strip = slice(row, row + STRIP)
        states = [got_ref[strip, :].astype(f32) for got_ref in gots]
        before = jnp.where(group == 1, far_ref[strip, :].astype(f32), 0.0)
        for r in range(half):
            total = before
            for other in range(half):
                if other != r:
                    total = total + jnp.where(sources[other] < sources[r], states[other], 0.0)
            backs[r][strip, :] = total.astype(bf16)


def shares_kernel(half, far_ref, *refs):
    gots, shares_ref = refs[:half], refs[half]
    part = gots[0].shape[0] - PAD
    group, place = lax.div(lax.axis_index("seq"), half), lax.rem(lax.axis_index("seq"), half)
    far = far_ref[part:, :].astype(f32)
    for r in range(half):
        source = lax.bitwise_xor(place, r)
        terms = gots[r][part:, :].astype(f32)
        shares_ref[group * half + source, 0:2, :] = terms[0:2] + terms[2:4]
        terms = far[4 * r : 4 * r + 4]
        shares_ref[(1 - group) * half + source, 0:2, :] = terms[0:2] + terms[2:4]


def local_kernel(q_ref, k_ref, v_ref, within_ref):
    rows, width = q_ref.shape
    causal = lax.broadcasted_iota(jnp.int32, (rows, rows), 0) >= lax.broadcasted_iota(
        jnp.int32, (rows, rows), 1
    )
    for h in range(width // HEAD_DIM):
        cols = slice(h * HEAD_DIM, (h + 1) * HEAD_DIM)
        v = v_ref[:, cols]
        scores = jnp.where(causal, dot(q_ref[:, cols], k_ref[:, cols], ((1,), (1,))), 0.0)
        high = scores.astype(bf16)
        low = (scores - high.astype(f32)).astype(bf16)
        within_ref[:, cols] = dot(high, v) + dot(low, v)


def attention_kernel(half, first, after_ref, q_ref, within_ref, hg_ref, fg_ref, *refs):
    del after_ref
    carried, (att_ref, normed_ref) = refs[:half], refs[half:]
    rows, width = att_ref.shape
    take = slice(first, first + rows)
    part = width // half
    feature_sq = jnp.zeros((rows, HEAD_DIM), f32)
    for r in range(half):
        part_of = lax.bitwise_xor(lax.rem(lax.axis_index("seq"), half), r)
        for h in range(0, part, HEAD_DIM):
            cols = pl.ds(pl.multiple_of(part_of * part + h, HEAD_DIM), HEAD_DIM)
            raw = within_ref[take, cols] + dot(q_ref[take, cols], carried[r][h : h + HEAD_DIM, :])
            mean_square = jnp.mean(raw * raw, axis=-1, keepdims=True)
            att = (raw * lax.rsqrt(mean_square + epsilon) * hg_ref[:, cols]).astype(bf16)
            att_ref[:, cols] = att
            att = att.astype(f32)
            feature_sq = feature_sq + att * att
    scale = lax.rsqrt(jnp.sum(feature_sq, axis=-1, keepdims=True) / width + epsilon)
    for h in range(width // HEAD_DIM):
        cols = slice(h * HEAD_DIM, (h + 1) * HEAD_DIM)
        normed_ref[:, cols] = (att_ref[:, cols].astype(f32) * scale * fg_ref[:, cols]).astype(bf16)


def expert_kernel(hop, w_ref, g0, u0, d0, g1, u1, d1, *refs):
    n_seq = w_ref.shape[0]
    seq, core = lax.axis_index("seq"), lax.axis_index("expert")
    last = n_seq - 1
    place = jnp.where(seq % 2 == 0, seq // 2, last - seq // 2)
    place = lax.rem(place + jnp.where(core == 0, n_seq - hop, hop), n_seq)
    source = jnp.where(2 * place < n_seq, 2 * place, 2 * (last - place) + 1)
    shares = jnp.transpose(w_ref[source])
    parts = len(refs) // 2
    x = jnp.concatenate([ref[...] for ref in refs[:parts]], axis=0)
    total = None
    for e, (g, u, d) in enumerate(((g0, u0, d0), (g1, u1, d1))):
        gate = dot(x, g[...])
        up = dot(x, u[...])
        hidden = (gate / (1.0 + jnp.exp(-gate)) * up * shares[:, e : e + 1]).astype(bf16)
        part = dot(hidden, d[...])
        total = part if total is None else total + part
    rows = total.shape[0] // parts
    for i, out_ref in enumerate(refs[parts:]):
        out_ref[...] = total[i * rows : (i + 1) * rows].astype(bf16)


def run_experts(hop, pieces, shares, weights):
    rows, width = pieces[0].shape
    hidden = weights[0].shape[1]
    count = len(pieces)
    return pl.pallas_call(
        functools.partial(expert_kernel, hop),
        in_specs=[VMEM] * (7 + count),
        out_specs=[VMEM] * count,
        out_shape=[jax.ShapeDtypeStruct((rows, width), bf16)] * count,
        compiler_params=pltpu.CompilerParams(vmem_limit_bytes=24 << 20),
        cost_estimate=pl.CostEstimate(
            flops=12 * count * rows * width * hidden,
            bytes_accessed=4 * count * rows * width,
            transcendentals=2 * count * rows * hidden,
        ),
        name="experts",
    )(shares, *weights, *pieces)


def in_hbm(*arrays):
    return [pltpu.with_memory_space_constraint(a, pltpu.HBM) for a in arrays]


def load_kernel(count, after_ref, *refs):
    del after_ref
    sems = refs[-1]
    copies = [pltpu.make_async_copy(refs[i], refs[count + i], sems.at[i]) for i in range(count)]
    for copy in copies:
        copy.start()
    for copy in copies:
        copy.wait()


def load(after, *arrays):
    arrays = in_hbm(*arrays)
    count = len(arrays)
    size = sum(a.size * a.dtype.itemsize for a in arrays)
    return pl.pallas_call(
        functools.partial(load_kernel, count),
        in_specs=[HBM] * (count + 1),
        out_specs=[VMEM] * count,
        out_shape=[jax.ShapeDtypeStruct(a.shape, a.dtype) for a in arrays],
        scratch_shapes=[pltpu.SemaphoreType.DMA((count,))],
        compiler_params=pltpu.CompilerParams(vmem_limit_bytes=1 << 20),
        cost_estimate=pl.CostEstimate(flops=0, bytes_accessed=size, transcendentals=0),
        name="load",
    )(after, *arrays)


def ring_of(n_seq):
    return list(range(0, n_seq, 2)) + list(range(n_seq - 1, 0, -2)) if n_seq > 1 else [0]


def per_device(
    n_seq,
    queries,
    key_rows,
    value_rows,
    head_gain,
    ffn_gain,
    expert_ids,
    router_weight,
    w_gate,
    w_up,
    w_down,
):
    _, rows, width = queries.shape
    q, k, v = queries[0], key_rows[0], value_rows[0]
    own = (w_gate[0], w_up[0], w_down[0])
    half = n_seq // 2

    ring = ring_of(n_seq)
    hops = []
    for i, s in enumerate(ring):
        hops.append((2 * s, 2 * ring[(i + 1) % n_seq]))
        hops.append((2 * s + 1, 2 * ring[i - 1] + 1))

    def hop(value):
        return lax.ppermute(value, ("seq", "expert"), hops)

    def along(blocks):
        moved = [blocks[0]]
        for r in range(1, half):
            pairs = [(s, s ^ r) for s in range(n_seq)]
            moved.append(lax.ppermute(blocks[r], "seq", pairs))
        return moved

    part = width // half
    sends = pl.pallas_call(
        functools.partial(state_kernel, half),
        in_specs=[HBM] * 4,
        out_specs=[VMEM] * half,
        scratch_shapes=[
            pltpu.VMEM((width, HEAD_DIM), bf16),
            pltpu.VMEM(expert_ids.shape[:0:-1], jnp.int32),
            pltpu.VMEM(expert_ids.shape[:0:-1], f32),
            pltpu.VMEM((rows, width), bf16),
            pltpu.VMEM((rows, width), bf16),
            pltpu.SemaphoreType.DMA((2 * CHUNKS + 2,)),
        ],
        compiler_params=SMALL,
        out_shape=[jax.ShapeDtypeStruct((part + PAD, HEAD_DIM), bf16)] * half,
        name="states",
    )(*in_hbm(expert_ids[0].T, router_weight[0].T, k, v))
    q, k, v, head_gain, ffn_gain = load(
        sends[0], q, k, v, head_gain.reshape(1, width), ffn_gain.reshape(1, width)
    )
    within = pl.pallas_call(
        local_kernel,
        in_specs=[VMEM] * 3,
        out_specs=VMEM,
        out_shape=jax.ShapeDtypeStruct((rows, width), f32),
        compiler_params=SMALL,
        cost_estimate=pl.CostEstimate(
            flops=6 * rows * rows * width, bytes_accessed=10 * rows * width, transcendentals=0
        ),
        name="local",
    )(q, k, v)
    own = load(sends[0], *own)
    other = [lax.ppermute(w, "expert", [(0, 1), (1, 0)]) for w in own]
    gots = along(sends)
    near = pl.pallas_call(
        functools.partial(total_kernel, half),
        in_specs=[ANY] + [VMEM] * half,
        out_specs=VMEM,
        compiler_params=SMALL,
        out_shape=jax.ShapeDtypeStruct((part + 4 * half, HEAD_DIM), bf16),
        name="total",
    )(own[0], *gots)
    far = lax.ppermute(near, "seq", [(s, (s + half) % n_seq) for s in range(n_seq)])
    backs = pl.pallas_call(
        functools.partial(prefix_kernel, half),
        in_specs=[ANY] + [VMEM] * (half + 1),
        out_specs=[VMEM] * half,
        compiler_params=SMALL,
        out_shape=[jax.ShapeDtypeStruct((part, HEAD_DIM), bf16)] * half,
        name="prefix",
    )(within, far, *gots)
    shares = pl.pallas_call(
        functools.partial(shares_kernel, half),
        in_specs=[VMEM] * (half + 1),
        out_specs=VMEM,
        compiler_params=SMALL,
        out_shape=jax.ShapeDtypeStruct((n_seq, 8, rows), f32),
        name="shares",
    )(far, *gots)
    carried = along(backs)
    piece = rows // PIECES
    attention, normed = [], []
    for i in range(PIECES):
        att_piece, normed_piece = pl.pallas_call(
            functools.partial(attention_kernel, half, i * piece),
            in_specs=[ANY] + [VMEM] * (half + 4),
            out_specs=[VMEM] * 2,
            compiler_params=SMALL,
            cost_estimate=pl.CostEstimate(
                flops=2 * piece * width * HEAD_DIM,
                bytes_accessed=2 * width * HEAD_DIM + 10 * piece * width,
                transcendentals=0,
            ),
            out_shape=[jax.ShapeDtypeStruct((piece, width), bf16)] * 2,
            name="attend",
        )(normed[-1] if normed else within, q, within, head_gain, ffn_gain, *carried)
        attention.append(att_piece)
        normed.append(normed_piece)
    weights = [*own, *other]

    held, partial, first = normed, None, None
    for step in range(n_seq):
        following = [hop(x) for x in held] if step < n_seq - 1 else held
        result = run_experts(step, held, shares, weights)
        if step == 0:
            first = result
        elif step == 1:
            partial = result
        else:
            partial = [hop(x) for x in partial]
            partial = [(p.astype(f32) + r.astype(f32)).astype(bf16) for p, r in zip(partial, result)]
        held = following
    partial = [hop(x) for x in partial]
    layer_out = [
        (a.astype(f32) + (p.astype(f32) + r.astype(f32))).astype(bf16)
        for a, p, r in zip(attention, partial, first)
    ]
    attention = jnp.concatenate(attention)[None]
    return attention, jnp.concatenate(layer_out)[None]


def solution(mesh):
    n_seq = mesh.shape["seq"]

    def body(*args):
        return per_device(n_seq, *args)

    tokens = P(("groups", "expert"), "seq", None)
    experts = P(("seq", "expert"), None, None)
    return jax.shard_map(
        body,
        mesh=mesh,
        in_specs=(tokens, tokens, tokens, P(), P(), tokens, tokens, experts, experts, experts),
        out_specs=(tokens, tokens),
        check_vma=False,
    )
```

```python
import functools

import jax
import jax.numpy as jnp
from jax import lax
from jax.experimental import pallas as pl
from jax.experimental.pallas import tpu as pltpu
from jax.sharding import PartitionSpec as P


HEAD_DIM = 128
PAD = 8
CHUNKS = 1
PIECES = 2
STRIP = 32

epsilon = 1e-06
f32 = jnp.float32
bf16 = jnp.bfloat16


VMEM = pl.BlockSpec(memory_space=pltpu.VMEM)
ANY = pl.BlockSpec(memory_space=pl.ANY)
HBM = pl.BlockSpec(memory_space=pltpu.HBM)
SMALL = pltpu.CompilerParams(vmem_limit_bytes=16 << 20)


def dot(a, b, dims=((1,), (0,))):
    return lax.dot_general(a, b, (dims, ((), ())), preferred_element_type=f32)


def state_kernel(half, ids_hbm, rw_hbm, k_hbm, v_hbm, *refs):
    sends, (state_ref, ids_ref, rw_ref, k_ref, v_ref, sems) = refs[:half], refs[half:]
    width = k_ref.shape[1]
    part = width // half
    chunk = width // CHUNKS
    copies = []
    for c in range(CHUNKS):
        cols = slice(c * chunk, (c + 1) * chunk)
        for i, (src, dst) in enumerate(((k_hbm, k_ref), (v_hbm, v_ref))):
            copies.append(pltpu.make_async_copy(src.at[:, cols], dst.at[:, cols], sems.at[2 * c + i]))
    copies.append(pltpu.make_async_copy(ids_hbm, ids_ref, sems.at[2 * CHUNKS]))
    copies.append(pltpu.make_async_copy(rw_hbm, rw_ref, sems.at[2 * CHUNKS + 1]))
    for copy in copies[-2:] + copies[:-2]:
        copy.start()
    copies[-2].wait()
    copies[-1].wait()
    group, place, core = lax.div(lax.axis_index("seq"), half), lax.rem(lax.axis_index("seq"), half), lax.axis_index("expert")
    ids = ids_ref[...]
    shares = rw_ref[...] / jnp.sum(rw_ref[...], axis=0, keepdims=True)

    def share_of(expert):
        return jnp.sum(jnp.where(ids == expert, shares, 0.0), axis=0, keepdims=True)

    for r, send_ref in enumerate(sends):
        to = lax.bitwise_xor(place, r)
        rows = []
        for side in (group, 1 - group):
            first = 2 * (side * half + to)
            both = jnp.concatenate([share_of(first + core), share_of(first + 1 - core)], axis=0)
            high = both.astype(bf16).astype(f32)
            rows += [high, both - high]
        send_ref[part:, :] = jnp.concatenate(rows, axis=0).astype(bf16)
    for c in range(CHUNKS):
        copies[2 * c].wait()
        copies[2 * c + 1].wait()
        for h in range(c * chunk // HEAD_DIM, (c + 1) * chunk // HEAD_DIM):
            cols = slice(h * HEAD_DIM, (h + 1) * HEAD_DIM)
            state_ref[cols, :] = dot(k_ref[:, cols], v_ref[:, cols], ((0,), (0,))).astype(bf16)
    for r, send_ref in enumerate(sends):
        to = lax.bitwise_xor(place, r)
        send_ref[:part, :] = state_ref[pl.ds(pl.multiple_of(to * part, part), part), :]


def total_kernel(half, after_ref, *refs):
    del after_ref
    gots, send_ref = refs[:half], refs[half]
    part = gots[0].shape[0] - PAD
    total = gots[0][:part, :].astype(f32)
    for r in range(1, half):
        total = total + gots[r][:part, :].astype(f32)
    send_ref[:part, :] = total.astype(bf16)
    terms = [got_ref[part:, :].astype(f32)[4:8] for got_ref in gots]
    send_ref[part:, :] = jnp.concatenate(terms, axis=0).astype(bf16)


def prefix_kernel(half, after_ref, far_ref, *refs):
    del after_ref
    gots, backs = refs[:half], refs[half:]
    part = backs[0].shape[0]
    group, place = lax.div(lax.axis_index("seq"), half), lax.rem(lax.axis_index("seq"), half)
    sources = [lax.bitwise_xor(place, r) for r in range(half)]
    for row in range(0, part, STRIP):
        strip = slice(row, row + STRIP)
        states = [got_ref[strip, :].astype(f32) for got_ref in gots]
        before = jnp.where(group == 1, far_ref[strip, :].astype(f32), 0.0)
        for r in range(half):
            total = before
            for other in range(half):
                if other != r:
                    total = total + jnp.where(sources[other] < sources[r], states[other], 0.0)
            backs[r][strip, :] = total.astype(bf16)


def shares_kernel(half, far_ref, *refs):
    gots, shares_ref = refs[:half], refs[half]
    part = gots[0].shape[0] - PAD
    group, place = lax.div(lax.axis_index("seq"), half), lax.rem(lax.axis_index("seq"), half)
    far = far_ref[part:, :].astype(f32)
    for r in range(half):
        source = lax.bitwise_xor(place, r)
        terms = gots[r][part:, :].astype(f32)
        shares_ref[group * half + source, 0:2, :] = terms[0:2] + terms[2:4]
        terms = far[4 * r : 4 * r + 4]
        shares_ref[(1 - group) * half + source, 0:2, :] = terms[0:2] + terms[2:4]


def local_kernel(q_ref, k_ref, v_ref, within_ref):
    rows, width = q_ref.shape
    causal = lax.broadcasted_iota(jnp.int32, (rows, rows), 0) >= lax.broadcasted_iota(
        jnp.int32, (rows, rows), 1
    )
    for h in range(width // HEAD_DIM):
        cols = slice(h * HEAD_DIM, (h + 1) * HEAD_DIM)
        v = v_ref[:, cols]
        scores = jnp.where(causal, dot(q_ref[:, cols], k_ref[:, cols], ((1,), (1,))), 0.0)
        high = scores.astype(bf16)
        low = (scores - high.astype(f32)).astype(bf16)
        within_ref[:, cols] = dot(high, v) + dot(low, v)


def attention_kernel(half, first, after_ref, q_ref, within_ref, hg_ref, fg_ref, *refs):
    del after_ref
    carried, (att_ref, normed_ref) = refs[:half], refs[half:]
    rows, width = att_ref.shape
    take = slice(first, first + rows)
    part = width // half
    feature_sq = jnp.zeros((rows, HEAD_DIM), f32)
    for r in range(half):
        part_of = lax.bitwise_xor(lax.rem(lax.axis_index("seq"), half), r)
        for h in range(0, part, HEAD_DIM):
            cols = pl.ds(pl.multiple_of(part_of * part + h, HEAD_DIM), HEAD_DIM)
            raw = within_ref[take, cols] + dot(q_ref[take, cols], carried[r][h : h + HEAD_DIM, :])
            mean_square = jnp.mean(raw * raw, axis=-1, keepdims=True)
            att = (raw * lax.rsqrt(mean_square + epsilon) * hg_ref[:, cols]).astype(bf16)
            att_ref[:, cols] = att
            att = att.astype(f32)
            feature_sq = feature_sq + att * att
    scale = lax.rsqrt(jnp.sum(feature_sq, axis=-1, keepdims=True) / width + epsilon)
    for h in range(width // HEAD_DIM):
        cols = slice(h * HEAD_DIM, (h + 1) * HEAD_DIM)
        normed_ref[:, cols] = (att_ref[:, cols].astype(f32) * scale * fg_ref[:, cols]).astype(bf16)


def expert_kernel(hop, w_ref, g0, u0, d0, g1, u1, d1, *refs):
    n_seq = w_ref.shape[0]
    seq, core = lax.axis_index("seq"), lax.axis_index("expert")
    last = n_seq - 1
    place = jnp.where(seq % 2 == 0, seq // 2, last - seq // 2)
    place = lax.rem(place + jnp.where(core == 0, n_seq - hop, hop), n_seq)
    source = jnp.where(2 * place < n_seq, 2 * place, 2 * (last - place) + 1)
    shares = jnp.transpose(w_ref[source])
    parts = len(refs) // 2
    x = jnp.concatenate([ref[...] for ref in refs[:parts]], axis=0)
    total = None
    for e, (g, u, d) in enumerate(((g0, u0, d0), (g1, u1, d1))):
        gate = dot(x, g[...])
        up = dot(x, u[...])
        hidden = (gate / (1.0 + jnp.exp(-gate)) * up * shares[:, e : e + 1]).astype(bf16)
        part = dot(hidden, d[...])
        total = part if total is None else total + part
    rows = total.shape[0] // parts
    for i, out_ref in enumerate(refs[parts:]):
        out_ref[...] = total[i * rows : (i + 1) * rows].astype(bf16)


def run_experts(hop, pieces, shares, weights):
    rows, width = pieces[0].shape
    hidden = weights[0].shape[1]
    count = len(pieces)
    return pl.pallas_call(
        functools.partial(expert_kernel, hop),
        in_specs=[VMEM] * (7 + count),
        out_specs=[VMEM] * count,
        out_shape=[jax.ShapeDtypeStruct((rows, width), bf16)] * count,
        compiler_params=pltpu.CompilerParams(vmem_limit_bytes=24 << 20),
        cost_estimate=pl.CostEstimate(
            flops=12 * count * rows * width * hidden,
            bytes_accessed=4 * count * rows * width,
            transcendentals=2 * count * rows * hidden,
        ),
        name="experts",
    )(shares, *weights, *pieces)


def in_hbm(*arrays):
    return [pltpu.with_memory_space_constraint(a, pltpu.HBM) for a in arrays]


def load_kernel(count, after_ref, *refs):
    del after_ref
    sems = refs[-1]
    copies = [pltpu.make_async_copy(refs[i], refs[count + i], sems.at[i]) for i in range(count)]
    for copy in copies:
        copy.start()
    for copy in copies:
        copy.wait()


def load(after, *arrays):
    arrays = in_hbm(*arrays)
    count = len(arrays)
    size = sum(a.size * a.dtype.itemsize for a in arrays)
    return pl.pallas_call(
        functools.partial(load_kernel, count),
        in_specs=[HBM] * (count + 1),
        out_specs=[VMEM] * count,
        out_shape=[jax.ShapeDtypeStruct(a.shape, a.dtype) for a in arrays],
        scratch_shapes=[pltpu.SemaphoreType.DMA((count,))],
        compiler_params=pltpu.CompilerParams(vmem_limit_bytes=1 << 20),
        cost_estimate=pl.CostEstimate(flops=0, bytes_accessed=size, transcendentals=0),
        name="load",
    )(after, *arrays)


def ring_of(n_seq):
    return list(range(0, n_seq, 2)) + list(range(n_seq - 1, 0, -2)) if n_seq > 1 else [0]


def per_device(
    n_seq,
    queries,
    key_rows,
    value_rows,
    head_gain,
    ffn_gain,
    expert_ids,
    router_weight,
    w_gate,
    w_up,
    w_down,
):
    _, rows, width = queries.shape
    q, k, v = queries[0], key_rows[0], value_rows[0]
    own = (w_gate[0], w_up[0], w_down[0])
    half = n_seq // 2

    ring = ring_of(n_seq)
    hops = []
    for i, s in enumerate(ring):
        hops.append((2 * s, 2 * ring[(i + 1) % n_seq]))
        hops.append((2 * s + 1, 2 * ring[i - 1] + 1))

    def hop(value):
        return lax.ppermute(value, ("seq", "expert"), hops)

    def along(blocks):
        moved = [blocks[0]]
        for r in range(1, half):
            pairs = [(s, s ^ r) for s in range(n_seq)]
            moved.append(lax.ppermute(blocks[r], "seq", pairs))
        return moved

    part = width // half
    sends = pl.pallas_call(
        functools.partial(state_kernel, half),
        in_specs=[HBM] * 4,
        out_specs=[VMEM] * half,
        scratch_shapes=[
            pltpu.VMEM((width, HEAD_DIM), bf16),
            pltpu.VMEM(expert_ids.shape[:0:-1], jnp.int32),
            pltpu.VMEM(expert_ids.shape[:0:-1], f32),
            pltpu.VMEM((rows, width), bf16),
            pltpu.VMEM((rows, width), bf16),
            pltpu.SemaphoreType.DMA((2 * CHUNKS + 2,)),
        ],
        compiler_params=SMALL,
        out_shape=[jax.ShapeDtypeStruct((part + PAD, HEAD_DIM), bf16)] * half,
        name="states",
    )(*in_hbm(expert_ids[0].T, router_weight[0].T, k, v))
    q, k, v, head_gain, ffn_gain = load(
        sends[0], q, k, v, head_gain.reshape(1, width), ffn_gain.reshape(1, width)
    )
    within = pl.pallas_call(
        local_kernel,
        in_specs=[VMEM] * 3,
        out_specs=VMEM,
        out_shape=jax.ShapeDtypeStruct((rows, width), f32),
        compiler_params=SMALL,
        cost_estimate=pl.CostEstimate(
            flops=6 * rows * rows * width, bytes_accessed=10 * rows * width, transcendentals=0
        ),
        name="local",
    )(q, k, v)
    own = load(sends[0], *own)
    other = []
    for w in own:
        other.append(lax.ppermute(w, "expert", [(0, 1), (1, 0)]))
    gots = along(sends)
    near = pl.pallas_call(
        functools.partial(total_kernel, half),
        in_specs=[ANY] + [VMEM] * half,
        out_specs=VMEM,
        compiler_params=SMALL,
        out_shape=jax.ShapeDtypeStruct((part + 4 * half, HEAD_DIM), bf16),
        name="total",
    )(own[0], *gots)
    far = lax.ppermute(near, "seq", [(s, (s + half) % n_seq) for s in range(n_seq)])
    backs = pl.pallas_call(
        functools.partial(prefix_kernel, half),
        in_specs=[ANY] + [VMEM] * (half + 1),
        out_specs=[VMEM] * half,
        compiler_params=SMALL,
        out_shape=[jax.ShapeDtypeStruct((part, HEAD_DIM), bf16)] * half,
        name="prefix",
    )(within, far, *gots)
    shares = pl.pallas_call(
        functools.partial(shares_kernel, half),
        in_specs=[VMEM] * (half + 1),
        out_specs=VMEM,
        compiler_params=SMALL,
        out_shape=jax.ShapeDtypeStruct((n_seq, 8, rows), f32),
        name="shares",
    )(far, *gots)
    carried = along(backs)
    piece = rows // PIECES
    attention, normed = [], []
    for i in range(PIECES):
        att_piece, normed_piece = pl.pallas_call(
            functools.partial(attention_kernel, half, i * piece),
            in_specs=[ANY] + [VMEM] * (half + 4),
            out_specs=[VMEM] * 2,
            compiler_params=SMALL,
            cost_estimate=pl.CostEstimate(
                flops=2 * piece * width * HEAD_DIM,
                bytes_accessed=2 * width * HEAD_DIM + 10 * piece * width,
                transcendentals=0,
            ),
            out_shape=[jax.ShapeDtypeStruct((piece, width), bf16)] * 2,
            name="attend",
        )(normed[-1] if normed else within, q, within, head_gain, ffn_gain, *carried)
        attention.append(att_piece)
        normed.append(normed_piece)
    weights = [*own, *other]

    held, partial, first = normed, None, None
    for step in range(n_seq):
        following = [hop(x) for x in held] if step < n_seq - 1 else held
        result = run_experts(step, held, shares, weights)
        if step == 0:
            first = result
        elif step == 1:
            partial = result
        else:
            partial = [hop(x) for x in partial]
            partial = [(p.astype(f32) + r.astype(f32)).astype(bf16) for p, r in zip(partial, result)]
        held = following
    partial = [hop(x) for x in partial]
    layer_out = [
        (a.astype(f32) + (p.astype(f32) + r.astype(f32))).astype(bf16)
        for a, p, r in zip(attention, partial, first)
    ]
    attention = jnp.concatenate(attention)[None]
    return attention, jnp.concatenate(layer_out)[None]


def solution(mesh):
    n_seq = mesh.shape["seq"]

    def body(*args):
        return per_device(n_seq, *args)

    tokens = P(("groups", "expert"), "seq", None)
    experts = P(("seq", "expert"), None, None)
    return jax.shard_map(
        body,
        mesh=mesh,
        in_specs=(tokens, tokens, tokens, P(), P(), tokens, tokens, experts, experts, experts),
        out_specs=(tokens, tokens),
        check_vma=False,
    )
```
